32 devices in a mesh: groups: 2 (over y), expert: 8 (over z, core), attn: 2 (over x).
Axes of the slice: x: 2, y: 2, z: 4, core: 2. Of those that a mesh axis runs over, the one named last changes fastest.
Arguments:
- tokens: bfloat16 [512, 3584], P(('groups', 'expert')), parts along dimension 0, may hold values from -6 to 6
- gates: float32 [512, 8], P(('groups', 'expert')), parts along dimension 0, may hold values from 0.05 to 0.6
- slots: int32 [512, 8], P(('groups', 'expert')), parts along dimension 0, may hold values from 0 to 15, all different within a row; in each aligned block of 32 rows (0 to 31, 32 to 63, ...) at most 20 rows name the same one
- plan: int32 [16], P('groups'), parts along dimension 0, may hold values from 0 to 7, as said below
- gate_proj: bfloat16 [8, 3584, 1024], P('expert', None, 'attn'), may hold values from -0.09375 to 0.09375
- up_proj: bfloat16 [8, 3584, 1024], P('expert', None, 'attn'), may hold values from -0.09375 to 0.09375
- down_proj: bfloat16 [8, 3584, 1024], P('expert', None, 'attn'), may hold values from -0.1875 to 0.1875
Outputs:
- moe_out: bfloat16 [512, 3584], P(('groups', 'expert')), parts along dimension 0
The draws below stay inside these ranges and needn't reach their ends.
There are 2 independent parts, one for each index of `groups`. The reference program is written for one: setup_inputs(seed, part) draws one part's arguments, and reference() takes and returns one part's arrays. A program takes and returns all parts, laid end to end along the dimension named above; an argument that names none is the same for every part. Nothing has to cross between parts.
Inputs may be any that keep to these rules, and one draw needn't show every extreme that they name: A row's 8 slots are distinct; among the 32 rows of one index of expert (aligned blocks) no slot is named more than 20 times, a bound that some block reaches. plan[d] is never d; no expert is named by more than 2 entries of plan, and some expert by exactly 2.
All inputs are finite; a program needn't handle non-finite values.
Results may differ from the reference program's by a relative error of at most 0.014.
Values may be sent and summed in bfloat16 or wider, within the bound.
A program may use at most 128 MiB of HBM per device.

```python
import math
import jax
import jax.numpy as jnp
import numpy as np
from jax import lax

D = 3584
FF = 1024
TOP = 8
TOK_DEV = 32
TOKENS = 256
EXPERTS = 8
SPARES = 8
SLOTS = 16
CAP = 20
N_EXPERT = 8
N_ATTN = 2


def draw_plan(key, part):
    order = jax.random.permutation(jax.random.fold_in(key, 11), SPARES).astype(jnp.int32)
    index = jnp.arange(SPARES, dtype=jnp.int32)
    half = SPARES // 2
    target = jnp.where(index < half, index // 2 * 2 + 2, (index + 1) % SPARES)
    result = jnp.zeros((SPARES,), jnp.int32).at[order].set(order[target])
    return result


def levels(stream_key, shape, shards, low, high):
    loudness = 1.0
    for axis_at, blocks in shards:
        draws = jax.random.uniform(jax.random.fold_in(jax.random.fold_in(stream_key, 6), axis_at), (blocks,), jnp.float32, low / len(shards), high / len(shards))
        loudness = loudness * jnp.repeat(jnp.exp(draws), shape[axis_at] // blocks).reshape((-1,) + (1,) * (len(shape) - 1 - axis_at))
    return loudness


def routed_block(rng, own, number, rows, count, top, limit, slope):
    order = jax.random.permutation(rng, count)
    packed, usual = portions_of(count, rows * top, limit, slope, True), portions_of(count, rows * top, limit, slope, False)
    places = jnp.arange(count)

    def named(lengths, rotation):
        used = int((lengths > 0).sum())
        fixed = max(1, used // 4)
        moved = fixed + (places - fixed + rotation * (used - fixed)) % max(1, count - fixed)
        return jnp.zeros((count,), jnp.int32).at[order[jnp.where(places < fixed, places, moved)]].set(jnp.asarray(lengths, jnp.int32))

    lengths = jnp.where(number % 4 == 0, named(packed, number // 4), named(usual, number - number // 4 - 1))
    mixed = jax.random.permutation(jax.random.fold_in(own, 3), count)
    giver, taker = mixed[0:count // 2 * 2:2], mixed[1:count // 2 * 2:2]
    margin = jnp.minimum(lengths[giver] - 1, limit - lengths[taker]) // 2
    margin = jnp.where((giver == order[0]) | (taker == order[0]) | (lengths[taker] == 0), 0, jnp.maximum(margin, 0))
    moved = jax.random.randint(jax.random.fold_in(own, 4), (count // 2,), 0, 1 << 20) % (margin + 1)
    lengths = lengths.at[giver].add(-moved).at[taker].add(moved)
    labels = jnp.searchsorted(jnp.cumsum(lengths), jnp.arange(rows * top), side="right").astype(jnp.int32)
    table = labels.reshape(top, rows).T
    table = table[jax.random.permutation(jax.random.fold_in(own, 1), rows)]
    rotation = jax.random.randint(jax.random.fold_in(own, 2), (rows, 1), 0, top)
    return jnp.take_along_axis(table, (jnp.arange(top)[None, :] + rotation) % top, axis=1)


def portions_of(amount, total, limit, skew, full):
    portions = [(1 << 20) // math.isqrt(grade ** skew) + 1 for grade in range(1, amount + 1)]
    largest = limit if full else min(limit, max(-(-total // amount), total * portions[0] // sum(portions)))
    least = 1 if total - largest >= amount - 1 else 0
    counts, spare = [largest] + [least] * (amount - 1), total - largest - least * (amount - 1)
    while spare > 0:
        free = [i for i in range(1, amount) if counts[i] < largest] or [i for i in range(1, amount) if counts[i] < limit]
        whole, budget = sum([portions[i] for i in free]), spare
        for i in free:
            more = min(limit - counts[i], max(1, budget * portions[i] // whole), spare)
            counts[i] = counts[i] + more
            spare = spare - more
    return np.array(counts)


def noise(key, extent, deviation, reach, pieces=(), kind=jnp.bfloat16):
    drawn = deviation * jax.random.normal(key, extent, jnp.float32)
    if pieces:
        drawn = drawn * levels(key, extent, pieces, -0.22, 0.18)
    return jnp.clip(drawn, -reach, reach).astype(kind)


def setup_inputs(seed: int = 0, part: int = 0) -> dict:
    streams_of = jax.random.split(jax.random.key(seed), 8)
    part_splits = jax.random.split(jax.random.fold_in(streams_of[7], part), 8)
    tokens = noise(part_splits[0], (TOKENS, D), 1.0, 6.0, ((0, 8),))
    gates = jnp.clip(jnp.exp(math.log(0.6) - 2.4849067 * jax.random.uniform(part_splits[1], (TOKENS, TOP), jnp.float32) ** levels(part_splits[1], (TOKENS, TOP), ((0, 8),), -0.2, 0.2)), 0.05, 0.6)
    slots_keys = jax.random.split(jax.random.fold_in(part_splits[2], 1), TOKENS // TOK_DEV)
    slots_turns = jax.random.permutation(jax.random.fold_in(part_splits[2], 3), TOKENS // TOK_DEV)
    slots = jax.vmap(lambda own, number: routed_block(jax.random.fold_in(part_splits[2], 2), own, number, TOK_DEV, SLOTS, TOP, CAP, 1))(slots_keys, slots_turns).reshape((TOKENS, TOP))
    plan = draw_plan(jax.random.fold_in(jax.random.fold_in(streams_of[7], part), 71), part)
    gate_proj = noise(streams_of[4], (EXPERTS, D, FF), D ** -0.5, 0.09375, ((0, 8), (2, 2)))
    up_proj = noise(streams_of[5], (EXPERTS, D, FF), D ** -0.5, 0.09375, ((0, 8), (2, 2)))
    down_proj = noise(streams_of[6], (EXPERTS, D, FF), FF ** -0.5, 0.1875, ((0, 8), (2, 2)))
    return dict(tokens=tokens, gates=gates, slots=slots, plan=plan, gate_proj=gate_proj, up_proj=up_proj, down_proj=down_proj)


def expert_rows(rows, w_gate, w_up, w_down):
    rows_float = rows.astype(jnp.float32)
    gate_act = jnp.dot(rows_float, w_gate.astype(jnp.float32), precision=lax.Precision.HIGHEST)
    up_act = jnp.dot(rows_float, w_up.astype(jnp.float32), precision=lax.Precision.HIGHEST)
    hidden = (jax.nn.silu(gate_act) * up_act).astype(jnp.bfloat16)
    row_count = rows.shape[0]
    group = FF // N_ATTN
    hidden_split = hidden.astype(jnp.float32).reshape(row_count, N_ATTN, group)
    down_split = w_down.astype(jnp.float32).reshape(D, N_ATTN, group)
    down_part = jnp.einsum("rap,dap->rad", hidden_split, down_split, precision=lax.Precision.HIGHEST)
    down_part = lax.optimization_barrier(down_part.astype(jnp.bfloat16))
    return jnp.sum(down_part.astype(jnp.float32), axis=1)


def reference(tokens, gates, slots, plan, gate_proj, up_proj, down_proj):
    slot_ids = jnp.arange(2 * N_EXPERT, dtype=jnp.int32)
    expert_of = jnp.where(slot_ids % 2 == 0, slot_ids // 2, plan[slot_ids // 2]).astype(jnp.int32)
    per_block = TOK_DEV * TOP
    pair_slots = slots.reshape(N_EXPERT, per_block).astype(jnp.int32)
    onehot = (pair_slots[:, :, None] == slot_ids[None, None, :]).astype(jnp.int32)
    running = jnp.cumsum(onehot, axis=1)
    position = (jnp.sum(running * onehot, axis=2) - 1).astype(jnp.int32)
    block_index = jnp.broadcast_to(jnp.arange(N_EXPERT, dtype=jnp.int32)[:, None], (N_EXPERT, per_block))
    local_token = jnp.broadcast_to((jnp.arange(per_block, dtype=jnp.int32) // TOP)[None, :], (N_EXPERT, per_block))
    token_table = jnp.zeros((2 * N_EXPERT, N_EXPERT, CAP), jnp.int32)
    token_table = token_table.at[pair_slots, block_index, position].set(local_token + block_index * TOK_DEV)

    def one_slot(slot):
        expert = expert_of[slot]
        rows = tokens[token_table[slot].reshape(-1)]
        result = expert_rows(rows, gate_proj[expert], up_proj[expert], down_proj[expert])
        return result.reshape(N_EXPERT, CAP, D)

    outputs = lax.map(one_slot, slot_ids)
    picked = outputs[pair_slots, block_index, position]
    picked = picked.reshape(N_EXPERT * TOK_DEV, TOP, D)
    total = jnp.sum(picked * gates[:, :, None], axis=1)
    return total.astype(jnp.bfloat16)
```

```python
import functools

import jax
import jax.numpy as jnp
from jax import lax
from jax.experimental import pallas as pl
from jax.experimental.pallas import tpu as pltpu
from jax.sharding import PartitionSpec as P

MESH = pl.DeviceIdType.MESH
LANES = 128
ROWS = 16
CHUNKS = 2


def combined_gates(gates, slots, plan, experts):
    choice = slots // 2
    expert = jnp.where(slots % 2 == 0, choice, plan[choice])
    ids = jnp.arange(experts, dtype=jnp.int32)
    return jnp.sum(jnp.where(expert[:, :, None] == ids, gates[:, :, None], 0.0), axis=1)


def dense_body(tokens, gates, slots, plan, gate_proj, up_proj, down_proj):
    experts = lax.axis_size("expert")
    weight = combined_gates(gates, slots, plan, experts)
    everyone = lax.all_gather(tokens, "expert", axis=0, tiled=True)
    weights = lax.all_to_all(weight, "expert", split_axis=1, concat_axis=0, tiled=True)
    gate_act = jnp.dot(everyone, gate_proj[0], preferred_element_type=jnp.float32)
    up_act = jnp.dot(everyone, up_proj[0], preferred_element_type=jnp.float32)
    hidden = (jax.nn.silu(gate_act) * up_act).astype(jnp.bfloat16)
    down = jnp.einsum("rf,df->rd", hidden, down_proj[0], preferred_element_type=jnp.float32)
    part = (down * weights).astype(jnp.bfloat16)
    part = lax.psum_scatter(part, "expert", scatter_dimension=0, tiled=True)
    return lax.psum(part, "attn")


def split_tiles(total, parts):
    tiles = total // LANES
    edges = [(tiles * p + parts - 1) // parts * LANES for p in range(parts + 1)]
    return [(a, b - a) for a, b in zip(edges, edges[1:]) if b > a]


def kernel(
    nz, chunks,
    tokens, gates_hbm, slots_hbm, plan_hbm, gate_hbm, up_hbm, down_hbm,
    out,
    gates, slots, plan, rows, wg, wu, wd, hid, hid_send, hid_recv, grow,
    keep, b_send, b_recv, c_send, c_recv, d_send,
    send_sem, local_sem, row_sem, g_sem, w_sem, h_sem, b_sem, c_sem, d_sem,
):
    f32, bf16 = jnp.float32, jnp.bfloat16
    experts = 2 * nz
    me = lax.axis_index("expert")
    x = lax.axis_index("attn")
    z, c = me // 2, me % 2
    tok, half = rows.shape[-2], rows.shape[-1]
    quarter = half // 2
    units = wg.shape[-1]
    both = 2 * tok
    mine = pl.ds(pl.multiple_of(x * half, LANES), half)
    other = pl.ds(pl.multiple_of((1 - x) * half, LANES), half)
    partner = {"expert": z * 2 + (1 - c)}
    across = {"attn": 1 - x}
    diagonal_peer = {"expert": z * 2 + (1 - c), "attn": 1 - x}

    barrier = pltpu.get_barrier_semaphore()

    def greet(peer):
        pl.semaphore_signal(barrier, inc=1, device_id=peer, device_id_type=MESH)

    greet(across)
    greet(partner)
    for step in (1, -1):
        pl.when((z + step >= 0) & (z + step < nz))(
            functools.partial(greet, {"expert": (z + step) * 2 + c})
        )

    counts = {"send": 0, "local": 0}
    pending = []

    def local(src, dst):
        copy = pltpu.make_async_copy(src, dst, local_sem.at[counts["local"]])
        counts["local"] += 1
        copy.start()
        return copy

    def prepare(src, dst, sem, device):
        copy = pltpu.make_async_remote_copy(
            src_ref=src, dst_ref=dst, send_sem=send_sem.at[counts["send"]], recv_sem=sem,
            device_id=device, device_id_type=MESH,
        )
        counts["send"] += 1
        return copy

    def send(src, dst, sem, device, when=None):
        copy = prepare(src, dst, sem, device)
        if when is None:
            copy.start()
        else:
            pl.when(when)(copy.start)
        pending.append((when, copy))

    def drain():
        while pending:
            when, copy = pending.pop(0)
            if when is None:
                copy.wait_send()
            else:
                pl.when(when)(copy.wait_send)

    def arrived(dst, sem):
        pltpu.make_async_remote_copy(
            src_ref=dst, dst_ref=dst, send_sem=send_sem.at[0], recv_sem=sem,
            device_id=partner, device_id_type=MESH,
        ).wait_recv()

    own_copies = [
        local(tokens.at[:, mine], rows.at[0, 0, 0]),
        local(tokens.at[:, other], rows.at[1, 0, 0]),
    ]
    small_copies = [local(gates_hbm, gates), local(slots_hbm, slots), local(plan_hbm, plan)]
    weight_copies = []
    for h, part in enumerate((mine, other)):
        weight_copies.append(local(gate_hbm.at[0, part, :], wg.at[h]))
        weight_copies.append(local(up_hbm.at[0, part, :], wu.at[h]))

    def down_rows(core, side):
        start = core * half + (x if side == 0 else 1 - x) * quarter
        return pl.ds(pl.multiple_of(start, LANES), quarter)

    down_copies = [
        local(down_hbm.at[0, down_rows(c, side), :], wd.at[0, side]) for side in (1, 0)
    ]

    for copy in small_copies:
        copy.wait()
    named = slots[...]
    expert = lax.shift_right_logical(named, 1)
    target = expert
    for d in range(experts):
        target = jnp.where(expert == d, plan[d], target)
    expert = jnp.where((named & 1) == 0, expert, target)
    gate = gates[...]
    for e in range(experts):
        grow[0, 0, e, :, :tok] = jnp.sum(jnp.where(expert == e, gate, 0.0), axis=0, keepdims=True)
    for copy in own_copies:
        copy.wait()

    pl.semaphore_wait(barrier, 2 + jnp.where(z > 0, 1, 0) + jnp.where(z < nz - 1, 1, 0))

    pieces = tok // ROWS
    cuts = [pl.ds(q * ROWS, ROWS) for q in range(pieces)]

    def step_of(at, origin):
        reach = jnp.minimum(at, nz - 1 - at)
        gap = jnp.abs(origin - at)
        near = 2 * gap - jnp.where(origin > at, 1, 0)
        return jnp.clip(jnp.where(gap <= reach, near, gap + reach), 0, nz - 1)

    def piece(h, r, slot, q):
        return rows.at[h, slot, r, cuts[q]], row_sem.at[h, r, slot, q]

    def weights_of(r, slot):
        return grow.at[r, slot], g_sem.at[r, slot]

    for q in range(pieces):
        for step in (1, -1):
            valid = (z + step >= 0) & (z + step < nz)
            there = {"expert": (z + step) * 2 + c}
            slot = step_of(z + step, z)
            send(piece(0, 0, 0, q)[0], *piece(0, 0, slot, q), there, valid)
            if q == 0:
                send(grow.at[0, 0], *weights_of(0, slot), there, valid)
    for h in range(2):
        send(rows.at[h, 0, 0], rows.at[h, 0, 1], row_sem.at[h, 1, 0, 0], partner)
    send(grow.at[0, 0], *weights_of(1, 0), partner)
    for side in (1, 0):
        send(down_hbm.at[0, down_rows(1 - c, side), :], wd.at[1, side], w_sem.at[side], partner)

    def from_z(hop, q):
        for step in (1, -1):
            origin = z - step * hop
            valid = (origin >= 0) & (origin < nz)
            onward = valid & (z + step >= 0) & (z + step < nz)
            there = {"expert": (z + step) * 2 + c}
            slot, further = step_of(z, origin), step_of(z + step, origin)
            block, sem = piece(0, 0, slot, q)
            pl.when(valid)(functools.partial(arrived, block, sem))
            send(block, *piece(1, 0, slot, q), across, valid)
            if hop < nz - 1:
                send(block, *piece(0, 0, further, q), there, onward)
            send(block, *piece(0, 1, slot, q), partner, valid)
            if q == 0:
                line, sem = weights_of(0, slot)
                pl.when(valid)(functools.partial(arrived, line, sem))
                if hop < nz - 1:
                    send(line, *weights_of(0, further), there, onward)
                send(line, *weights_of(1, slot), partner, valid)

    def from_across(hop, q):
        for step in (1, -1):
            origin = z - step * hop
            valid = (origin >= 0) & (origin < nz)
            slot = step_of(z, origin)
            block, sem = piece(1, 0, slot, q)
            pl.when(valid)(functools.partial(arrived, block, sem))
            send(block, *piece(1, 1, slot, q), partner, valid)

    reach = jnp.minimum(z, nz - 1 - z)
    toward = jnp.where(2 * z < nz, 1, -1)

    def origin_of(s):
        if s == 0:
            return z
        near = z + (s + 1) // 2 * (1 if s % 2 else -1)
        return jnp.clip(jnp.where(s <= 2 * reach, near, z + toward * (s - reach)), 0, nz - 1)

    origins = [origin_of(s) for s in range(nz)]
    tile = 256 if units % 256 == 0 else LANES
    tiles = [pl.ds(t * tile, tile) for t in range(units // tile)]
    eye = lax.broadcasted_iota(jnp.int32, (tok, LANES), 0) == lax.broadcasted_iota(
        jnp.int32, (tok, LANES), 1
    )

    def ready(s):
        if s:
            for h in range(2):
                for q in range(pieces):
                    arrived(*piece(h, 1, s, q))
        else:
            for h in range(2):
                arrived(rows.at[h, 0, 1], row_sem.at[h, 1, 0, 0])
        arrived(*weights_of(1, s))

    def up(first, count, t):
        cols = tiles[t]
        at = pl.ds(first, count)

        def product(weights):
            return jnp.dot(
                rows[0, at].reshape(count * both, half), weights[0, :, cols],
                preferred_element_type=f32,
            ) + jnp.dot(
                rows[1, at].reshape(count * both, half), weights[1, :, cols],
                preferred_element_type=f32,
            )

        scale = jnp.concatenate(
            [
                jnp.sum(jnp.where(eye, grow[r, s, me], 0.0), axis=1, keepdims=True)
                for s in range(first, first + count)
                for r in range(2)
            ],
            axis=0,
        )
        gate_act, up_act = product(wg), product(wu)
        value = gate_act / (1.0 + jnp.exp(-gate_act)) * up_act * scale
        value = value.astype(bf16).reshape(count, both, tile)
        hid[at, :, cols] = value
        hid_send[at, :tok, cols] = value[:, tok:]
        hid_send[at, tok:, cols] = value[:, :tok]

    def share(first, count):
        at = pl.ds(first, count)
        send(hid_send.at[at], hid_recv.at[at], h_sem.at[first], partner)

    def hidden(first, count):
        arrived(hid_recv.at[pl.ds(first, count)], h_sem.at[first])

    def down(first, count, side, n):
        at, cols = pl.ds(first, count), pl.ds(*chunks[n])
        value = sum(
            lax.dot_general(
                source[at].reshape(count * both, units), wd[which, side, cols, :],
                (((1,), (1,)), ((), ())), preferred_element_type=f32,
            )
            for which, source in enumerate((hid, hid_recv))
        ).reshape(count, both, chunks[n][1])
        if side == 0:
            keep[at, :, cols] = value
        else:
            b_send[at, :, cols] = value.astype(bf16)

    def release(s, n):
        cols = pl.ds(*chunks[n])
        send(b_send.at[s, :, cols], b_recv.at[s, :, cols], b_sem.at[s, n], across)

    def reduced(s, n):
        cols = pl.ds(*chunks[n])
        arrived(b_recv.at[s, :, cols], b_sem.at[s, n])
        value = keep[s, :, cols] + b_recv[s, :, cols].astype(f32)
        if s == 0:
            keep[s, :, cols] = value
        else:
            c_send[s - 1, :, cols] = value.astype(bf16)
            send(
                c_send.at[s - 1, :, cols], c_recv.at[z, :, cols], c_sem.at[z, n],
                {"expert": origins[s] * 2 + c},
            )

    def weights_of_down():
        for copy in down_copies:
            copy.wait()
        for side in (1, 0):
            arrived(wd.at[1, side], w_sem.at[side])

    order = range(len(chunks))
    last = nz - 1
    waves = [(first, min(2, nz - first)) for first in range(0, nz, 2)]

    def gate_and_up(wave):
        first, count = waves[wave]
        for s in range(first, first + count):
            ready(s)
        if wave == 0:
            for copy in weight_copies:
                copy.wait()
        for t in range(len(tiles)):
            up(first, count, t)
        share(first, count)

    def down_out(wave):
        first, count = waves[wave]
        hidden(first, count)
        if wave == 0:
            weights_of_down()
        for n in order:
            down(first, count, 1, n)
            release(first + count - 1, n)
        for s in range(first + count - 2, first - 1, -1):
            for n in order:
                release(s, n)

    def down_kept(wave):
        first, count = waves[wave]
        for n in order:
            down(first, count, 0, n)

    for q in range(pieces):
        from_z(1, q)
    for hop in range(2, last):
        for q in range(pieces):
            from_z(hop, q)
            from_across(hop - 1, q)
    if last > 1:
        from_z(last, 0)
        if last == 2:
            from_across(1, 0)
            for q in range(1, pieces):
                from_z(last, q)
                from_across(1, q)
            gate_and_up(0)
        else:
            gate_and_up(0)
            from_across(last - 1, 0)
            for q in range(1, pieces):
                from_z(last, q)
        down_out(0)
        down_kept(0)
        if last > 2:
            for q in range(1, pieces):
                from_across(last - 1, q)
        for q in range(pieces):
            from_across(last, q)
    else:
        for q in range(pieces):
            from_across(1, q)
        gate_and_up(0)
        down_out(0)
        down_kept(0)
    for wave in range(1, len(waves)):
        gate_and_up(wave)
        down_out(wave)
        first, count = waves[wave - 1]
        for s in range(first + count - 1, max(first, 1) - 1, -1):
            for n in order:
                reduced(s, n)
        down_kept(wave)
    first, count = waves[-1]
    for s in range(first + count - 1, max(first, 1) - 1, -1):
        for n in order:
            reduced(s, n)
    for n in order:
        reduced(0, n)

    base = c * half + x * quarter
    out_copies = []
    for n, (at, width) in enumerate(chunks):
        cols = pl.ds(at, width)
        value = keep[0, :, cols]
        for s in range(1, nz):
            slot = origins[s]
            arrived(c_recv.at[slot, :, cols], c_sem.at[slot, n])
            value = value + c_recv[slot, :, cols].astype(f32)
        d_send[:, cols] = value.astype(bf16)
        target = pl.ds(pl.multiple_of(base + at, LANES), width)
        near, far = d_send.at[:tok, cols], d_send.at[tok:, cols]
        send(far, out.at[:, target], d_sem.at[2, n], diagonal_peer)
        send(near, out.at[:, target], d_sem.at[0, n], across)
        send(far, out.at[:, target], d_sem.at[1, n], partner)
        out_copies.append(local(near, out.at[:, target]))

    for n, (at, width) in enumerate(chunks):
        for which, (core, side) in enumerate(((c, 1 - x), (1 - c, x), (1 - c, 1 - x))):
            start = pl.multiple_of(core * half + side * quarter + at, LANES)
            arrived(out.at[:, pl.ds(start, width)], d_sem.at[which, n])
    for copy in out_copies:
        copy.wait()
    drain()


def fused_body(tokens, gates, slots, plan, gate_proj, up_proj, down_proj):
    f32, bf16 = jnp.float32, jnp.bfloat16
    nz = lax.axis_size("expert") // 2
    tok, model = tokens.shape
    top = gates.shape[1]
    half = model // 2
    quarter = half // 2
    units = gate_proj.shape[2]
    both = 2 * tok
    pieces = tok // ROWS
    chunks = split_tiles(quarter, CHUNKS)
    many = len(chunks)
    dma = pltpu.SemaphoreType.DMA
    anywhere = pl.BlockSpec(memory_space=pl.ANY)
    sends = 8 * nz * pieces + 4 * nz + 8 + nz + many * (2 * nz + 3)
    return pl.pallas_call(
        functools.partial(kernel, nz, chunks),
        out_shape=jax.ShapeDtypeStruct((tok, model), bf16),
        in_specs=[anywhere] * 7,
        out_specs=anywhere,
        scratch_shapes=[
            pltpu.VMEM((top, tok), f32),
            pltpu.VMEM((top, tok), jnp.int32),
            pltpu.SMEM(plan.shape, jnp.int32),
            pltpu.VMEM((2, nz, 2, tok, half), bf16),
            pltpu.VMEM((2, half, units), bf16),
            pltpu.VMEM((2, half, units), bf16),
            pltpu.VMEM((2, 2, quarter, units), bf16),
            pltpu.VMEM((nz, both, units), bf16),
            pltpu.VMEM((nz, both, units), bf16),
            pltpu.VMEM((nz, both, units), bf16),
            pltpu.VMEM((2, nz, 2 * nz, 1, LANES), f32),
            pltpu.VMEM((nz, both, quarter), f32),
            pltpu.VMEM((nz, both, quarter), bf16),
            pltpu.VMEM((nz, both, quarter), bf16),
            pltpu.VMEM((nz - 1, both, quarter), bf16),
            pltpu.VMEM((nz, both, quarter), bf16),
            pltpu.VMEM((both, quarter), bf16),
            dma((sends,)),
            dma((11 + many,)),
            dma((2, 2, nz, pieces)),
            dma((2, nz)),
            dma((2,)),
            dma((nz,)),
            dma((nz, many)),
            dma((nz, many)),
            dma((3, many)),
        ],
        compiler_params=pltpu.CompilerParams(
            collective_id=0, has_side_effects=True
        ),
    )(tokens, gates.T, slots.T, plan, gate_proj, up_proj, down_proj)


def body(tokens, gates, slots, plan, gate_proj, up_proj, down_proj):
    experts, attn = lax.axis_size("expert"), lax.axis_size("attn")
    tok, model = tokens.shape
    fits = (
        attn == 2 and experts % 2 == 0 and experts > 2
        and tok % ROWS == 0 and tok <= LANES
        and model % (4 * LANES) == 0 and gate_proj.shape[0] == 1
        and gate_proj.shape[2] % LANES == 0
    )
    chosen = fused_body if fits else dense_body
    return chosen(tokens, gates, slots, plan, gate_proj, up_proj, down_proj)


def solution(mesh):
    return jax.shard_map(
        body,
        mesh=mesh,
        in_specs=(
            P(("groups", "expert"), None),
            P(("groups", "expert"), None),
            P(("groups", "expert"), None),
            P("groups"),
            P("expert", None, "attn"),
            P("expert", None, "attn"),
            P("expert", None, "attn"),
        ),
        out_specs=P(("groups", "expert"), None),
        check_vma=False,
    )
```

```python
import functools

import jax
import jax.numpy as jnp
from jax import lax
from jax.experimental import pallas as pl
from jax.experimental.pallas import tpu as pltpu
from jax.sharding import PartitionSpec as P

MESH = pl.DeviceIdType.MESH
LANES = 128
ROWS = 16
CHUNKS = 2


def combined_gates(gates, slots, plan, experts):
    choice = slots // 2
    expert = jnp.where(slots % 2 == 0, choice, plan[choice])
    ids = jnp.arange(experts, dtype=jnp.int32)
    return jnp.sum(jnp.where(expert[:, :, None] == ids, gates[:, :, None], 0.0), axis=1)


def dense_body(tokens, gates, slots, plan, gate_proj, up_proj, down_proj):
    experts = lax.axis_size("expert")
    weight = combined_gates(gates, slots, plan, experts)
    everyone = lax.all_gather(tokens, "expert", axis=0, tiled=True)
    weights = lax.all_to_all(weight, "expert", split_axis=1, concat_axis=0, tiled=True)
    gate_act = jnp.dot(everyone, gate_proj[0], preferred_element_type=jnp.float32)
    up_act = jnp.dot(everyone, up_proj[0], preferred_element_type=jnp.float32)
    hidden = (jax.nn.silu(gate_act) * up_act).astype(jnp.bfloat16)
    down = jnp.einsum("rf,df->rd", hidden, down_proj[0], preferred_element_type=jnp.float32)
    part = (down * weights).astype(jnp.bfloat16)
    part = lax.psum_scatter(part, "expert", scatter_dimension=0, tiled=True)
    return lax.psum(part, "attn")


def split_tiles(total, parts):
    tiles = total // LANES
    edges = [(tiles * p + parts - 1) // parts * LANES for p in range(parts + 1)]
    return [(a, b - a) for a, b in zip(edges, edges[1:]) if b > a]


def kernel(
    nz, chunks,
    tokens, gates_hbm, slots_hbm, plan_hbm, gate_hbm, up_hbm, down_hbm,
    out,
    gates, slots, plan, rows, wg, wu, wd, hid, hid_send, hid_recv, grow,
    keep, b_send, b_recv, c_send, c_recv, d_send,
    send_sem, local_sem, row_sem, g_sem, w_sem, h_sem, b_sem, c_sem, d_sem,
):
    f32, bf16 = jnp.float32, jnp.bfloat16
    experts = 2 * nz
    me = lax.axis_index("expert")
    x = lax.axis_index("attn")
    z, c = me // 2, me % 2
    tok, half = rows.shape[-2], rows.shape[-1]
    quarter = half // 2
    units = wg.shape[-1]
    both = 2 * tok
    mine = pl.ds(pl.multiple_of(x * half, LANES), half)
    other = pl.ds(pl.multiple_of((1 - x) * half, LANES), half)
    partner = {"expert": z * 2 + (1 - c)}
    across = {"attn": 1 - x}
    diagonal_peer = {"expert": z * 2 + (1 - c), "attn": 1 - x}

    barrier = pltpu.get_barrier_semaphore()

    def greet(peer):
        pl.semaphore_signal(barrier, inc=1, device_id=peer, device_id_type=MESH)

    greet(across)
    greet(partner)
    for step in (1, -1):
        pl.when((z + step >= 0) & (z + step < nz))(
            functools.partial(greet, {"expert": (z + step) * 2 + c})
        )

    counts = {"send": 0, "local": 0}
    pending = []

    def local(src, dst):
        copy = pltpu.make_async_copy(src, dst, local_sem.at[counts["local"]])
        counts["local"] += 1
        copy.start()
        return copy

    def prepare(src, dst, sem, device):
        copy = pltpu.make_async_remote_copy(
            src_ref=src, dst_ref=dst, send_sem=send_sem.at[counts["send"]], recv_sem=sem,
            device_id=device, device_id_type=MESH,
        )
        counts["send"] += 1
        return copy

    def send(src, dst, sem, device, when=None):
        copy = prepare(src, dst, sem, device)
        if when is None:
            copy.start()
        else:
            pl.when(when)(copy.start)
        pending.append((when, copy))

    def drain():
        while pending:
            when, copy = pending.pop(0)
            if when is None:
                copy.wait_send()
            else:
                pl.when(when)(copy.wait_send)

    def arrived(dst, sem):
        pltpu.make_async_remote_copy(
            src_ref=dst, dst_ref=dst, send_sem=send_sem.at[0], recv_sem=sem,
            device_id=partner, device_id_type=MESH,
        ).wait_recv()

    own_copies = [
        local(tokens.at[:, mine], rows.at[0, 0, 0]),
        local(tokens.at[:, other], rows.at[1, 0, 0]),
    ]
    small_copies = [local(gates_hbm, gates), local(slots_hbm, slots), local(plan_hbm, plan)]
    weight_copies = []
    for h, part in enumerate((mine, other)):
        weight_copies.append(local(gate_hbm.at[0, part, :], wg.at[h]))
        weight_copies.append(local(up_hbm.at[0, part, :], wu.at[h]))

    def down_rows(core, side):
        start = core * half + (x if side == 0 else 1 - x) * quarter
        return pl.ds(pl.multiple_of(start, LANES), quarter)

    down_copies = [
        local(down_hbm.at[0, down_rows(c, side), :], wd.at[0, side]) for side in (1, 0)
    ]

    for copy in small_copies:
        copy.wait()
    named = slots[...]
    expert = lax.shift_right_logical(named, 1)
    target = expert
    for d in range(experts):
        target = jnp.where(expert == d, plan[d], target)
    expert = jnp.where((named & 1) == 0, expert, target)
    gate = gates[...]
    for e in range(experts):
        grow[0, 0, e, :, :tok] = jnp.sum(jnp.where(expert == e, gate, 0.0), axis=0, keepdims=True)
    for copy in own_copies:
        copy.wait()

    pl.semaphore_wait(barrier, 2 + jnp.where(z > 0, 1, 0) + jnp.where(z < nz - 1, 1, 0))

    pieces = tok // ROWS
    cuts = [pl.ds(q * ROWS, ROWS) for q in range(pieces)]

    def step_of(at, origin):
        reach = jnp.minimum(at, nz - 1 - at)
        gap = jnp.abs(origin - at)
        inward = jnp.where(2 * at < nz, origin - at, at - origin)
        near = 2 * gap - jnp.where(inward > 0, 1, 0)
        return jnp.clip(jnp.where(gap <= reach, near, gap + reach), 0, nz - 1)

    def piece(h, r, slot, q):
        return rows.at[h, slot, r, cuts[q]], row_sem.at[h, r, slot, q]

    def weights_of(r, slot):
        return grow.at[r, slot], g_sem.at[r, slot]

    for q in range(pieces):
        for step in (1, -1):
            valid = (z + step >= 0) & (z + step < nz)
            there = {"expert": (z + step) * 2 + c}
            slot = step_of(z + step, z)
            send(piece(0, 0, 0, q)[0], *piece(0, 0, slot, q), there, valid)
            if q == 0:
                send(grow.at[0, 0], *weights_of(0, slot), there, valid)
    for h in range(2):
        send(rows.at[h, 0, 0], rows.at[h, 0, 1], row_sem.at[h, 1, 0, 0], partner)
    send(grow.at[0, 0], *weights_of(1, 0), partner)
    for side in (1, 0):
        send(down_hbm.at[0, down_rows(1 - c, side), :], wd.at[1, side], w_sem.at[side], partner)

    def from_z(hop, q):
        for step in (1, -1):
            origin = z - step * hop
            valid = (origin >= 0) & (origin < nz)
            onward = valid & (z + step >= 0) & (z + step < nz)
            there = {"expert": (z + step) * 2 + c}
            slot, further = step_of(z, origin), step_of(z + step, origin)
            block, sem = piece(0, 0, slot, q)
            pl.when(valid)(functools.partial(arrived, block, sem))
            send(block, *piece(1, 0, slot, q), across, valid)
            if hop < nz - 1:
                send(block, *piece(0, 0, further, q), there, onward)
            send(block, *piece(0, 1, slot, q), partner, valid)
            if q == 0:
                line, sem = weights_of(0, slot)
                pl.when(valid)(functools.partial(arrived, line, sem))
                if hop < nz - 1:
                    send(line, *weights_of(0, further), there, onward)
                send(line, *weights_of(1, slot), partner, valid)

    def from_across(hop, q):
        for step in (1, -1):
            origin = z - step * hop
            valid = (origin >= 0) & (origin < nz)
            slot = step_of(z, origin)
            block, sem = piece(1, 0, slot, q)
            pl.when(valid)(functools.partial(arrived, block, sem))
            send(block, *piece(1, 1, slot, q), partner, valid)

    reach = jnp.minimum(z, nz - 1 - z)
    toward = jnp.where(2 * z < nz, 1, -1)

    def origin_of(s):
        if s == 0:
            return z
        near = z + (s + 1) // 2 * (toward if s % 2 else -toward)
        return jnp.clip(jnp.where(s <= 2 * reach, near, z + toward * (s - reach)), 0, nz - 1)

    origins = [origin_of(s) for s in range(nz)]
    tile = 256 if units % 256 == 0 else LANES
    tiles = [pl.ds(t * tile, tile) for t in range(units // tile)]
    eye = lax.broadcasted_iota(jnp.int32, (tok, LANES), 0) == lax.broadcasted_iota(
        jnp.int32, (tok, LANES), 1
    )

    def ready(s):
        if s:
            for h in range(2):
                for q in range(pieces):
                    arrived(*piece(h, 1, s, q))
        else:
            for h in range(2):
                arrived(rows.at[h, 0, 1], row_sem.at[h, 1, 0, 0])
        arrived(*weights_of(1, s))

    def up(first, count, t):
        cols = tiles[t]
        at = pl.ds(first, count)

        def product(weights):
            return jnp.dot(
                rows[0, at].reshape(count * both, half), weights[0, :, cols],
                preferred_element_type=f32,
            ) + jnp.dot(
                rows[1, at].reshape(count * both, half), weights[1, :, cols],
                preferred_element_type=f32,
            )

        scale = jnp.concatenate(
            [
                jnp.sum(jnp.where(eye, grow[r, s, me], 0.0), axis=1, keepdims=True)
                for s in range(first, first + count)
                for r in range(2)
            ],
            axis=0,
        )
        gate_act, up_act = product(wg), product(wu)
        value = gate_act / (1.0 + jnp.exp(-gate_act)) * up_act * scale
        value = value.astype(bf16).reshape(count, both, tile)
        hid[at, :, cols] = value
        hid_send[at, :tok, cols] = value[:, tok:]
        hid_send[at, tok:, cols] = value[:, :tok]

    def share(first, count):
        at = pl.ds(first, count)
        send(hid_send.at[at], hid_recv.at[at], h_sem.at[first], partner)

    def hidden(first, count):
        arrived(hid_recv.at[pl.ds(first, count)], h_sem.at[first])

    def down(first, count, side, n):
        at, cols = pl.ds(first, count), pl.ds(*chunks[n])
        value = sum(
            lax.dot_general(
                source[at].reshape(count * both, units), wd[which, side, cols, :],
                (((1,), (1,)), ((), ())), preferred_element_type=f32,
            )
            for which, source in enumerate((hid, hid_recv))
        ).reshape(count, both, chunks[n][1])
        if side == 0:
            keep[at, :, cols] = value
        else:
            b_send[at, :, cols] = value.astype(bf16)

    def release(s, n):
        cols = pl.ds(*chunks[n])
        send(b_send.at[s, :, cols], b_recv.at[s, :, cols], b_sem.at[s, n], across)

    def reduced(s, n):
        cols = pl.ds(*chunks[n])
        arrived(b_recv.at[s, :, cols], b_sem.at[s, n])
        value = keep[s, :, cols] + b_recv[s, :, cols].astype(f32)
        if s == 0:
            keep[s, :, cols] = value
        else:
            c_send[s - 1, :, cols] = value.astype(bf16)
            send(
                c_send.at[s - 1, :, cols], c_recv.at[z, :, cols], c_sem.at[z, n],
                {"expert": origins[s] * 2 + c},
            )

    def weights_of_down():
        for copy in down_copies:
            copy.wait()
        for side in (1, 0):
            arrived(wd.at[1, side], w_sem.at[side])

    order = range(len(chunks))
    last = nz - 1
    waves = [(first, min(2, nz - first)) for first in range(0, nz, 2)]

    def gate_and_up(wave):
        first, count = waves[wave]
        for s in range(first, first + count):
            ready(s)
        if wave == 0:
            for copy in weight_copies:
                copy.wait()
        for t in range(len(tiles)):
            up(first, count, t)
        share(first, count)

    def down_out(wave):
        first, count = waves[wave]
        hidden(first, count)
        if wave == 0:
            weights_of_down()
        for n in order:
            down(first, count, 1, n)
            release(first + count - 1, n)
        for s in range(first + count - 2, first - 1, -1):
            for n in order:
                release(s, n)

    def down_kept(wave):
        first, count = waves[wave]
        for n in order:
            down(first, count, 0, n)

    for q in range(pieces):
        from_z(1, q)
    for hop in range(2, last):
        for q in range(pieces):
            from_z(hop, q)
            from_across(hop - 1, q)
    if last > 1:
        from_z(last, 0)
        if last == 2:
            from_across(1, 0)
            for q in range(1, pieces):
                from_z(last, q)
                from_across(1, q)
            gate_and_up(0)
        else:
            gate_and_up(0)
            from_across(last - 1, 0)
            for q in range(1, pieces):
                from_z(last, q)
        down_out(0)
        down_kept(0)
        if last > 2:
            for q in range(1, pieces):
                from_across(last - 1, q)
        for q in range(pieces):
            from_across(last, q)
    else:
        for q in range(pieces):
            from_across(1, q)
        gate_and_up(0)
        down_out(0)
        down_kept(0)
    for wave in range(1, len(waves)):
        gate_and_up(wave)
        down_out(wave)
        first, count = waves[wave - 1]
        for s in range(first + count - 1, max(first, 1) - 1, -1):
            for n in order:
                reduced(s, n)
        down_kept(wave)
    first, count = waves[-1]
    for s in range(first + count - 1, max(first, 1) - 1, -1):
        for n in order:
            reduced(s, n)
    for n in order:
        reduced(0, n)

    base = c * half + x * quarter
    out_copies = []
    for n, (at, width) in enumerate(chunks):
        cols = pl.ds(at, width)
        value = keep[0, :, cols]
        for s in range(1, nz):
            slot = origins[s]
            arrived(c_recv.at[slot, :, cols], c_sem.at[slot, n])
            value = value + c_recv[slot, :, cols].astype(f32)
        d_send[:, cols] = value.astype(bf16)
        target = pl.ds(pl.multiple_of(base + at, LANES), width)
        near, far = d_send.at[:tok, cols], d_send.at[tok:, cols]
        send(far, out.at[:, target], d_sem.at[2, n], diagonal_peer)
        send(near, out.at[:, target], d_sem.at[0, n], across)
        send(far, out.at[:, target], d_sem.at[1, n], partner)
        out_copies.append(local(near, out.at[:, target]))

    for n, (at, width) in enumerate(chunks):
        for which, (core, side) in enumerate(((c, 1 - x), (1 - c, x), (1 - c, 1 - x))):
            start = pl.multiple_of(core * half + side * quarter + at, LANES)
            arrived(out.at[:, pl.ds(start, width)], d_sem.at[which, n])
    for copy in out_copies:
        copy.wait()
    drain()


def fused_body(tokens, gates, slots, plan, gate_proj, up_proj, down_proj):
    f32, bf16 = jnp.float32, jnp.bfloat16
    nz = lax.axis_size("expert") // 2
    tok, model = tokens.shape
    top = gates.shape[1]
    half = model // 2
    quarter = half // 2
    units = gate_proj.shape[2]
    both = 2 * tok
    pieces = tok // ROWS
    chunks = split_tiles(quarter, CHUNKS)
    many = len(chunks)
    dma = pltpu.SemaphoreType.DMA
    anywhere = pl.BlockSpec(memory_space=pl.ANY)
    sends = 8 * nz * pieces + 4 * nz + 8 + nz + many * (2 * nz + 3)
    return pl.pallas_call(
        functools.partial(kernel, nz, chunks),
        out_shape=jax.ShapeDtypeStruct((tok, model), bf16),
        in_specs=[anywhere] * 7,
        out_specs=anywhere,
        scratch_shapes=[
            pltpu.VMEM((top, tok), f32),
            pltpu.VMEM((top, tok), jnp.int32),
            pltpu.SMEM(plan.shape, jnp.int32),
            pltpu.VMEM((2, nz, 2, tok, half), bf16),
            pltpu.VMEM((2, half, units), bf16),
            pltpu.VMEM((2, half, units), bf16),
            pltpu.VMEM((2, 2, quarter, units), bf16),
            pltpu.VMEM((nz, both, units), bf16),
            pltpu.VMEM((nz, both, units), bf16),
            pltpu.VMEM((nz, both, units), bf16),
            pltpu.VMEM((2, nz, 2 * nz, 1, LANES), f32),
            pltpu.VMEM((nz, both, quarter), f32),
            pltpu.VMEM((nz, both, quarter), bf16),
            pltpu.VMEM((nz, both, quarter), bf16),
            pltpu.VMEM((nz - 1, both, quarter), bf16),
            pltpu.VMEM((nz, both, quarter), bf16),
            pltpu.VMEM((both, quarter), bf16),
            dma((sends,)),
            dma((11 + many,)),
            dma((2, 2, nz, pieces)),
            dma((2, nz)),
            dma((2,)),
            dma((nz,)),
            dma((nz, many)),
            dma((nz, many)),
            dma((3, many)),
        ],
        compiler_params=pltpu.CompilerParams(
            collective_id=0, has_side_effects=True, vmem_limit_bytes=48 * 1024 * 1024
        ),
    )(*(pltpu.with_memory_space_constraint(a, pltpu.HBM) for a in (tokens, gates.T, slots.T, plan, gate_proj, up_proj, down_proj)))


def body(tokens, gates, slots, plan, gate_proj, up_proj, down_proj):
    experts, attn = lax.axis_size("expert"), lax.axis_size("attn")
    tok, model = tokens.shape
    fits = (
        attn == 2 and experts % 2 == 0 and experts > 2
        and tok % ROWS == 0 and tok <= LANES
        and model % (4 * LANES) == 0 and gate_proj.shape[0] == 1
        and gate_proj.shape[2] % LANES == 0
    )
    chosen = fused_body if fits else dense_body
    return chosen(tokens, gates, slots, plan, gate_proj, up_proj, down_proj)


def solution(mesh):
    return jax.shard_map(
        body,
        mesh=mesh,
        in_specs=(
            P(("groups", "expert"), None),
            P(("groups", "expert"), None),
            P(("groups", "expert"), None),
            P("groups"),
            P("expert", None, "attn"),
            P("expert", None, "attn"),
            P("expert", None, "attn"),
        ),
        out_specs=P(("groups", "expert"), None),
        check_vma=False,
    )
```

```python
import functools

import jax
import jax.numpy as jnp
from jax import lax
from jax.experimental import pallas as pl
from jax.experimental.pallas import tpu as pltpu
from jax.sharding import PartitionSpec as P

MESH = pl.DeviceIdType.MESH
LANES = 128
ROWS = 16
CHUNKS = 2


def combined_gates(gates, slots, plan, experts):
    choice = slots // 2
    expert = jnp.where(slots % 2 == 0, choice, plan[choice])
    ids = jnp.arange(experts, dtype=jnp.int32)
    return jnp.sum(jnp.where(expert[:, :, None] == ids, gates[:, :, None], 0.0), axis=1)


def dense_body(tokens, gates, slots, plan, gate_proj, up_proj, down_proj):
    experts = lax.axis_size("expert")
    weight = combined_gates(gates, slots, plan, experts)
    everyone = lax.all_gather(tokens, "expert", axis=0, tiled=True)
    weights = lax.all_to_all(weight, "expert", split_axis=1, concat_axis=0, tiled=True)
    gate_act = jnp.dot(everyone, gate_proj[0], preferred_element_type=jnp.float32)
    up_act = jnp.dot(everyone, up_proj[0], preferred_element_type=jnp.float32)
    hidden = (jax.nn.silu(gate_act) * up_act).astype(jnp.bfloat16)
    down = jnp.einsum("rf,df->rd", hidden, down_proj[0], preferred_element_type=jnp.float32)
    part = (down * weights).astype(jnp.bfloat16)
    part = lax.psum_scatter(part, "expert", scatter_dimension=0, tiled=True)
    return lax.psum(part, "attn")


def split_tiles(total, parts):
    tiles = total // LANES
    edges = [(tiles * p + parts - 1) // parts * LANES for p in range(parts + 1)]
    return [(a, b - a) for a, b in zip(edges, edges[1:]) if b > a]


def kernel(
    nz, chunks,
    tokens, gates_hbm, slots_hbm, plan_hbm, gate_hbm, up_hbm, down_hbm,
    out,
    gates, slots, plan, rows, wg, wu, wd, hid, hid_send, hid_recv, grow,
    early, ahead, keep, b_send, b_recv, c_send, c_recv, d_send,
    send_sem, local_sem, row_sem, g_sem, w_sem, h_sem, b_sem, c_sem, d_sem,
):
    f32, bf16 = jnp.float32, jnp.bfloat16
    experts = 2 * nz
    me = lax.axis_index("expert")
    x = lax.axis_index("attn")
    z, c = me // 2, me % 2
    tok, half = rows.shape[-2], rows.shape[-1]
    quarter = half // 2
    units = wg.shape[-1]
    both = 2 * tok
    mine = pl.ds(pl.multiple_of(x * half, LANES), half)
    other = pl.ds(pl.multiple_of((1 - x) * half, LANES), half)
    partner = {"expert": z * 2 + (1 - c)}
    across = {"attn": 1 - x}
    diagonal_peer = {"expert": z * 2 + (1 - c), "attn": 1 - x}

    barrier = pltpu.get_barrier_semaphore()

    def greet(peer):
        pl.semaphore_signal(barrier, inc=1, device_id=peer, device_id_type=MESH)

    greet(across)
    greet(partner)
    for step in (1, -1):
        pl.when((z + step >= 0) & (z + step < nz))(
            functools.partial(greet, {"expert": (z + step) * 2 + c})
        )

    counts = {"send": 0, "local": 0}
    pending = []

    def local(src, dst):
        copy = pltpu.make_async_copy(src, dst, local_sem.at[counts["local"]])
        counts["local"] += 1
        copy.start()
        return copy

    def prepare(src, dst, sem, device):
        copy = pltpu.make_async_remote_copy(
            src_ref=src, dst_ref=dst, send_sem=send_sem.at[counts["send"]], recv_sem=sem,
            device_id=device, device_id_type=MESH,
        )
        counts["send"] += 1
        return copy

    def send(src, dst, sem, device, when=None):
        copy = prepare(src, dst, sem, device)
        if when is None:
            copy.start()
        else:
            pl.when(when)(copy.start)
        pending.append((when, copy))

    def drain():
        while pending:
            when, copy = pending.pop(0)
            if when is None:
                copy.wait_send()
            else:
                pl.when(when)(copy.wait_send)

    def arrived(dst, sem):
        pltpu.make_async_remote_copy(
            src_ref=dst, dst_ref=dst, send_sem=send_sem.at[0], recv_sem=sem,
            device_id=partner, device_id_type=MESH,
        ).wait_recv()

    own_copies = [
        local(tokens.at[:, mine], rows.at[0, 0, 0]),
        local(tokens.at[:, other], rows.at[1, 0, 0]),
    ]
    small_copies = [local(gates_hbm, gates), local(slots_hbm, slots), local(plan_hbm, plan)]
    weight_copies = []
    for h, part in enumerate((mine, other)):
        weight_copies.append(local(gate_hbm.at[0, part, :], wg.at[h]))
        weight_copies.append(local(up_hbm.at[0, part, :], wu.at[h]))

    def down_rows(core, side):
        start = core * half + (x if side == 0 else 1 - x) * quarter
        return pl.ds(pl.multiple_of(start, LANES), quarter)

    down_copies = [
        local(down_hbm.at[0, down_rows(c, side), :], wd.at[0, side]) for side in (1, 0)
    ]

    for copy in small_copies:
        copy.wait()
    named = slots[...]
    expert = lax.shift_right_logical(named, 1)
    target = expert
    for d in range(experts):
        target = jnp.where(expert == d, plan[d], target)
    expert = jnp.where((named & 1) == 0, expert, target)
    gate = gates[...]
    for e in range(experts):
        grow[0, 0, e, :, :tok] = jnp.sum(jnp.where(expert == e, gate, 0.0), axis=0, keepdims=True)
    for copy in own_copies:
        copy.wait()

    pl.semaphore_wait(barrier, 2 + jnp.where(z > 0, 1, 0) + jnp.where(z < nz - 1, 1, 0))

    pieces = tok // ROWS
    cuts = [pl.ds(q * ROWS, ROWS) for q in range(pieces)]

    def step_of(at, origin):
        reach = jnp.minimum(at, nz - 1 - at)
        gap = jnp.abs(origin - at)
        inward = jnp.where(2 * at < nz, origin - at, at - origin)
        near = 2 * gap - jnp.where(inward > 0, 1, 0)
        return jnp.clip(jnp.where(gap <= reach, near, gap + reach), 0, nz - 1)

    def piece(h, r, slot, q):
        return rows.at[h, slot, r, cuts[q]], row_sem.at[h, r, slot, q]

    def weights_of(r, slot):
        return grow.at[r, slot], g_sem.at[r, slot]

    for q in range(pieces):
        for step in (1, -1):
            valid = (z + step >= 0) & (z + step < nz)
            there = {"expert": (z + step) * 2 + c}
            slot = step_of(z + step, z)
            send(piece(0, 0, 0, q)[0], *piece(0, 0, slot, q), there, valid)
            if q == 0:
                send(grow.at[0, 0], *weights_of(0, slot), there, valid)
    for h in range(2):
        send(rows.at[h, 0, 0], rows.at[h, 0, 1], row_sem.at[h, 1, 0, 0], partner)
    send(grow.at[0, 0], *weights_of(1, 0), partner)
    for side in (1, 0):
        send(down_hbm.at[0, down_rows(1 - c, side), :], wd.at[1, side], w_sem.at[side], partner)

    def from_z(hop, q):
        for step in (1, -1):
            origin = z - step * hop
            valid = (origin >= 0) & (origin < nz)
            onward = valid & (z + step >= 0) & (z + step < nz)
            there = {"expert": (z + step) * 2 + c}
            slot, further = step_of(z, origin), step_of(z + step, origin)
            block, sem = piece(0, 0, slot, q)
            pl.when(valid)(functools.partial(arrived, block, sem))
            send(block, *piece(1, 0, slot, q), across, valid)
            if hop < nz - 1:
                send(block, *piece(0, 0, further, q), there, onward)
            send(block, *piece(0, 1, slot, q), partner, valid)
            if q == 0:
                line, sem = weights_of(0, slot)
                pl.when(valid)(functools.partial(arrived, line, sem))
                if hop < nz - 1:
                    send(line, *weights_of(0, further), there, onward)
                send(line, *weights_of(1, slot), partner, valid)

    def from_across(hop, q):
        for step in (1, -1):
            origin = z - step * hop
            valid = (origin >= 0) & (origin < nz)
            slot = step_of(z, origin)
            block, sem = piece(1, 0, slot, q)
            pl.when(valid)(functools.partial(arrived, block, sem))
            send(block, *piece(1, 1, slot, q), partner, valid)

    reach = jnp.minimum(z, nz - 1 - z)
    toward = jnp.where(2 * z < nz, 1, -1)

    def origin_of(s):
        if s == 0:
            return z
        near = z + (s + 1) // 2 * (toward if s % 2 else -toward)
        return jnp.clip(jnp.where(s <= 2 * reach, near, z + toward * (s - reach)), 0, nz - 1)

    origins = [origin_of(s) for s in range(nz)]
    tile = 256 if units % 256 == 0 else LANES
    tiles = [pl.ds(t * tile, tile) for t in range(units // tile)]
    eye = lax.broadcasted_iota(jnp.int32, (tok, LANES), 0) == lax.broadcasted_iota(
        jnp.int32, (tok, LANES), 1
    )

    def ready(s, h):
        if s:
            for q in range(pieces):
                arrived(*piece(h, 1, s, q))
        else:
            arrived(rows.at[h, 0, 1], row_sem.at[h, 1, 0, 0])
        if h == 0:
            arrived(*weights_of(1, s))

    def product(first, count, h, weights, cols):
        return jnp.dot(
            rows[h, pl.ds(first, count)].reshape(count * both, half), weights[h, :, cols],
            preferred_element_type=f32,
        )

    def up_first_half(first, count):
        for s in range(first, first + count):
            ready(s, 0)
        for cols in tiles:
            early[0, : count * both, cols] = product(first, count, 0, wg, cols)
            early[1, : count * both, cols] = product(first, count, 0, wu, cols)

    def up(first, count, t):
        cols = tiles[t]
        at = pl.ds(first, count)

        scale = jnp.concatenate(
            [
                jnp.sum(jnp.where(eye, grow[r, s, me], 0.0), axis=1, keepdims=True)
                for s in range(first, first + count)
                for r in range(2)
            ],
            axis=0,
        )
        gate_act = early[0, : count * both, cols] + product(first, count, 1, wg, cols)
        up_act = early[1, : count * both, cols] + product(first, count, 1, wu, cols)
        value = gate_act / (1.0 + jnp.exp(-gate_act)) * up_act * scale
        value = value.astype(bf16).reshape(count, both, tile)
        hid[at, :, cols] = value
        hid_send[at, :tok, cols] = value[:, tok:]
        hid_send[at, tok:, cols] = value[:, :tok]

    def share(first, count):
        at = pl.ds(first, count)
        send(hid_send.at[at], hid_recv.at[at], h_sem.at[first], partner)

    def hidden(first, count):
        arrived(hid_recv.at[pl.ds(first, count)], h_sem.at[first])

    order = range(len(chunks))

    def down_product(source, which, first, count, side, cols):
        return lax.dot_general(
            source[pl.ds(first, count)].reshape(count * both, units), wd[which, side, cols, :],
            (((1,), (1,)), ((), ())), preferred_element_type=f32,
        )

    def down_own(first, count):
        for side in (1, 0):
            for n in order:
                cols = pl.ds(*chunks[n])
                ahead[side, : count * both, cols] = down_product(hid, 0, first, count, side, cols)

    def down(first, count, side, n):
        at, cols = pl.ds(first, count), pl.ds(*chunks[n])
        value = ahead[side, : count * both, cols] + down_product(
            hid_recv, 1, first, count, side, cols
        )
        value = value.reshape(count, both, chunks[n][1])
        if side == 0:
            keep[at, :, cols] = value
        else:
            b_send[at, :, cols] = value.astype(bf16)

    def release(s, n):
        cols = pl.ds(*chunks[n])
        send(b_send.at[s, :, cols], b_recv.at[s, :, cols], b_sem.at[s, n], across)

    def reduced(s, n, origin):
        cols = pl.ds(*chunks[n])
        arrived(b_recv.at[s, :, cols], b_sem.at[s, n])
        value = keep[s, :, cols] + b_recv[s, :, cols].astype(f32)
        if origin is None:
            keep[s, :, cols] = value
        else:
            c_send[s - 1, :, cols] = value.astype(bf16)
            send(
                c_send.at[s - 1, :, cols], c_recv.at[z, :, cols], c_sem.at[z, n],
                {"expert": origin * 2 + c},
            )

    def weights_of_down():
        for side in (1, 0):
            arrived(wd.at[1, side], w_sem.at[side])

    last = nz - 1
    waves = [(first, min(2, nz - first)) for first in range(0, nz, 2)]

    def begin(wave):
        first, count = waves[wave]
        if wave == 0:
            for copy in weight_copies:
                copy.wait()
        up_first_half(first, count)

    def gate_and_up(wave):
        first, count = waves[wave]
        for s in range(first, first + count):
            ready(s, 1)
        for t in range(len(tiles)):
            up(first, count, t)
        share(first, count)
        if wave == 0:
            for copy in down_copies:
                copy.wait()
        down_own(first, count)

    def own(s):
        return isinstance(s, int) and s == 0

    def turns(wave):
        first, count = waves[wave]
        if wave == 0 or count == 1:
            return [(s, origins[s]) for s in range(first + count - 1, first - 1, -1)]
        low = jnp.minimum(origins[first], origins[first + 1])
        high = jnp.maximum(origins[first], origins[first + 1])
        sooner = jnp.where(origins[first] < origins[first + 1], first, first + 1)
        return [(sooner, low), (2 * first + 1 - sooner, high)]

    def down_out(wave):
        first, count = waves[wave]
        hidden(first, count)
        if wave == 0:
            weights_of_down()
        for n in order:
            down(first, count, 1, n)
            release(turns(wave)[0][0], n)
        for s, _ in turns(wave)[1:]:
            for n in order:
                if not own(s):
                    release(s, n)
        if wave == len(waves) - 1:
            for n in order:
                release(0, n)

    def down_kept(wave):
        first, count = waves[wave]
        for n in order:
            down(first, count, 0, n)

    for q in range(pieces):
        from_z(1, q)
    for hop in range(2, last):
        for q in range(pieces):
            from_z(hop, q)
            from_across(hop - 1, q)
    if last > 1:
        from_z(last, 0)
        if last == 2:
            from_across(1, 0)
            for q in range(1, pieces):
                from_z(last, q)
                from_across(1, q)
            begin(0)
            gate_and_up(0)
        else:
            begin(0)
            gate_and_up(0)
            from_across(last - 1, 0)
            for q in range(1, pieces):
                from_z(last, q)
        down_out(0)
        down_kept(0)
        if last > 2:
            for q in range(1, pieces):
                from_across(last - 1, q)
        if len(waves) > 1:
            begin(1)
        for q in range(pieces):
            from_across(last, q)
    else:
        for q in range(pieces):
            from_across(1, q)
        begin(0)
        gate_and_up(0)
        down_out(0)
        down_kept(0)
    for wave in range(1, len(waves)):
        if wave > 1 or last < 2:
            begin(wave)
        gate_and_up(wave)
        down_out(wave)
        for s, origin in turns(wave - 1):
            for n in order:
                if not own(s):
                    reduced(s, n, origin)
        down_kept(wave)
    for s, origin in turns(len(waves) - 1):
        for n in order:
            if not own(s):
                reduced(s, n, origin)
    for n in order:
        reduced(0, n, None)

    base = c * half + x * quarter
    out_copies = []
    for n, (at, width) in enumerate(chunks):
        cols = pl.ds(at, width)
        value = keep[0, :, cols]
        for s in range(1, nz):
            slot = origins[s]
            arrived(c_recv.at[slot, :, cols], c_sem.at[slot, n])
            value = value + c_recv[slot, :, cols].astype(f32)
        d_send[:, cols] = value.astype(bf16)
        target = pl.ds(pl.multiple_of(base + at, LANES), width)
        near, far = d_send.at[:tok, cols], d_send.at[tok:, cols]
        send(far, out.at[:, target], d_sem.at[2, n], diagonal_peer)
        send(near, out.at[:, target], d_sem.at[0, n], across)
        send(far, out.at[:, target], d_sem.at[1, n], partner)
        out_copies.append(local(near, out.at[:, target]))

    for n, (at, width) in enumerate(chunks):
        for which, (core, side) in enumerate(((c, 1 - x), (1 - c, x), (1 - c, 1 - x))):
            start = pl.multiple_of(core * half + side * quarter + at, LANES)
            arrived(out.at[:, pl.ds(start, width)], d_sem.at[which, n])
    for copy in out_copies:
        copy.wait()
    drain()


def fused_body(tokens, gates, slots, plan, gate_proj, up_proj, down_proj):
    f32, bf16 = jnp.float32, jnp.bfloat16
    nz = lax.axis_size("expert") // 2
    tok, model = tokens.shape
    top = gates.shape[1]
    half = model // 2
    quarter = half // 2
    units = gate_proj.shape[2]
    both = 2 * tok
    pieces = tok // ROWS
    chunks = split_tiles(quarter, CHUNKS)
    many = len(chunks)
    dma = pltpu.SemaphoreType.DMA
    anywhere = pl.BlockSpec(memory_space=pl.ANY)
    sends = 8 * nz * pieces + 4 * nz + 8 + nz + many * (2 * nz + 3)
    return pl.pallas_call(
        functools.partial(kernel, nz, chunks),
        out_shape=jax.ShapeDtypeStruct((tok, model), bf16),
        in_specs=[anywhere] * 7,
        out_specs=anywhere,
        scratch_shapes=[
            pltpu.VMEM((top, tok), f32),
            pltpu.VMEM((top, tok), jnp.int32),
            pltpu.SMEM(plan.shape, jnp.int32),
            pltpu.VMEM((2, nz, 2, tok, half), bf16),
            pltpu.VMEM((2, half, units), bf16),
            pltpu.VMEM((2, half, units), bf16),
            pltpu.VMEM((2, 2, quarter, units), bf16),
            pltpu.VMEM((nz, both, units), bf16),
            pltpu.VMEM((nz, both, units), bf16),
            pltpu.VMEM((nz, both, units), bf16),
            pltpu.VMEM((2, nz, 2 * nz, 1, LANES), f32),
            pltpu.VMEM((2, 2 * both, units), f32),
            pltpu.VMEM((2, 2 * both, quarter), f32),
            pltpu.VMEM((nz, both, quarter), f32),
            pltpu.VMEM((nz, both, quarter), bf16),
            pltpu.VMEM((nz, both, quarter), bf16),
            pltpu.VMEM((nz - 1, both, quarter), bf16),
            pltpu.VMEM((nz, both, quarter), bf16),
            pltpu.VMEM((both, quarter), bf16),
            dma((sends,)),
            dma((11 + many,)),
            dma((2, 2, nz, pieces)),
            dma((2, nz)),
            dma((2,)),
            dma((nz,)),
            dma((nz, many)),
            dma((nz, many)),
            dma((3, many)),
        ],
        compiler_params=pltpu.CompilerParams(
            collective_id=0, has_side_effects=True, vmem_limit_bytes=48 * 1024 * 1024
        ),
    )(*(pltpu.with_memory_space_constraint(a, pltpu.HBM) for a in (tokens, gates.T, slots.T, plan, gate_proj, up_proj, down_proj)))


def body(tokens, gates, slots, plan, gate_proj, up_proj, down_proj):
    experts, attn = lax.axis_size("expert"), lax.axis_size("attn")
    tok, model = tokens.shape
    fits = (
        attn == 2 and experts % 2 == 0 and experts > 2
        and tok % ROWS == 0 and tok <= LANES
        and model % (4 * LANES) == 0 and gate_proj.shape[0] == 1
        and gate_proj.shape[2] % LANES == 0
    )
    chosen = fused_body if fits else dense_body
    return chosen(tokens, gates, slots, plan, gate_proj, up_proj, down_proj)


def solution(mesh):
    return jax.shard_map(
        body,
        mesh=mesh,
        in_specs=(
            P(("groups", "expert"), None),
            P(("groups", "expert"), None),
            P(("groups", "expert"), None),
            P("groups"),
            P("expert", None, "attn"),
            P("expert", None, "attn"),
            P("expert", None, "attn"),
        ),
        out_specs=P(("groups", "expert"), None),
        check_vma=False,
    )
```

```python
import functools

import jax
import jax.numpy as jnp
from jax import lax
from jax.experimental import pallas as pl
from jax.experimental.pallas import tpu as pltpu
from jax.sharding import PartitionSpec as P

MESH = pl.DeviceIdType.MESH
LANES = 128
ROWS = 16
CHUNKS = 2


def combined_gates(gates, slots, plan, experts):
    choice = slots // 2
    expert = jnp.where(slots % 2 == 0, choice, plan[choice])
    ids = jnp.arange(experts, dtype=jnp.int32)
    return jnp.sum(jnp.where(expert[:, :, None] == ids, gates[:, :, None], 0.0), axis=1)


def dense_body(tokens, gates, slots, plan, gate_proj, up_proj, down_proj):
    experts = lax.axis_size("expert")
    weight = combined_gates(gates, slots, plan, experts)
    everyone = lax.all_gather(tokens, "expert", axis=0, tiled=True)
    weights = lax.all_to_all(weight, "expert", split_axis=1, concat_axis=0, tiled=True)
    gate_act = jnp.dot(everyone, gate_proj[0], preferred_element_type=jnp.float32)
    up_act = jnp.dot(everyone, up_proj[0], preferred_element_type=jnp.float32)
    hidden = (jax.nn.silu(gate_act) * up_act).astype(jnp.bfloat16)
    down = jnp.einsum("rf,df->rd", hidden, down_proj[0], preferred_element_type=jnp.float32)
    part = (down * weights).astype(jnp.bfloat16)
    part = lax.psum_scatter(part, "expert", scatter_dimension=0, tiled=True)
    return lax.psum(part, "attn")


def split_tiles(total, parts):
    tiles = total // LANES
    edges = [(tiles * p + parts - 1) // parts * LANES for p in range(parts + 1)]
    return [(a, b - a) for a, b in zip(edges, edges[1:]) if b > a]


def kernel(
    nz, chunks,
    tokens, gates_hbm, slots_hbm, plan_hbm, gate_hbm, up_hbm, down_hbm,
    out,
    gates, slots, plan, rows, wg, wu, wd, hid, hid_send, hid_recv, grow,
    early, ahead, keep, b_send, b_recv, c_send, c_recv, d_send,
    send_sem, local_sem, row_sem, g_sem, w_sem, h_sem, b_sem, c_sem, d_sem,
):
    f32, bf16 = jnp.float32, jnp.bfloat16
    experts = 2 * nz
    me = lax.axis_index("expert")
    x = lax.axis_index("attn")
    z, c = me // 2, me % 2
    tok, half = rows.shape[-2], rows.shape[-1]
    quarter = half // 2
    units = wg.shape[-1]
    both = 2 * tok
    mine = pl.ds(pl.multiple_of(x * half, LANES), half)
    other = pl.ds(pl.multiple_of((1 - x) * half, LANES), half)
    partner = {"expert": z * 2 + (1 - c)}
    across = {"attn": 1 - x}
    diagonal_peer = {"expert": z * 2 + (1 - c), "attn": 1 - x}

    barrier = pltpu.get_barrier_semaphore()

    def greet(peer):
        pl.semaphore_signal(barrier, inc=1, device_id=peer, device_id_type=MESH)

    greet(across)
    greet(partner)
    for step in (1, -1):
        pl.when((z + step >= 0) & (z + step < nz))(
            functools.partial(greet, {"expert": (z + step) * 2 + c})
        )

    counts = {"send": 0, "local": 0}
    pending = []

    def local(src, dst):
        copy = pltpu.make_async_copy(src, dst, local_sem.at[counts["local"]])
        counts["local"] += 1
        copy.start()
        return copy

    def prepare(src, dst, sem, device):
        copy = pltpu.make_async_remote_copy(
            src_ref=src, dst_ref=dst, send_sem=send_sem.at[counts["send"]], recv_sem=sem,
            device_id=device, device_id_type=MESH,
        )
        counts["send"] += 1
        return copy

    def send(src, dst, sem, device, when=None):
        copy = prepare(src, dst, sem, device)
        if when is None:
            copy.start()
        else:
            pl.when(when)(copy.start)
        pending.append((when, copy))

    def drain(count):
        for _ in range(count):
            when, copy = pending.pop(0)
            if when is None:
                copy.wait_send()
            else:
                pl.when(when)(copy.wait_send)

    def arrived(dst, sem):
        pltpu.make_async_remote_copy(
            src_ref=dst, dst_ref=dst, send_sem=send_sem.at[0], recv_sem=sem,
            device_id=partner, device_id_type=MESH,
        ).wait_recv()

    own_copies = [
        local(tokens.at[:, mine], rows.at[0, 0, 0]),
        local(tokens.at[:, other], rows.at[1, 0, 0]),
    ]
    small_copies = [local(gates_hbm, gates), local(slots_hbm, slots), local(plan_hbm, plan)]
    weight_copies = []
    for h, part in enumerate((mine, other)):
        weight_copies.append(local(gate_hbm.at[0, part, :], wg.at[h]))
        weight_copies.append(local(up_hbm.at[0, part, :], wu.at[h]))

    def down_rows(core, side):
        start = core * half + (x if side == 0 else 1 - x) * quarter
        return pl.ds(pl.multiple_of(start, LANES), quarter)

    down_copies = [
        local(down_hbm.at[0, down_rows(c, side), :], wd.at[0, side]) for side in (1, 0)
    ]

    for copy in small_copies:
        copy.wait()
    named = slots[...]
    expert = lax.shift_right_logical(named, 1)
    target = expert
    for d in range(experts):
        target = jnp.where(expert == d, plan[d], target)
    expert = jnp.where((named & 1) == 0, expert, target)
    gate = gates[...]
    for e in range(experts):
        grow[0, 0, e, :, :tok] = jnp.sum(jnp.where(expert == e, gate, 0.0), axis=0, keepdims=True)
    for copy in own_copies:
        copy.wait()

    pl.semaphore_wait(barrier, 2 + jnp.where(z > 0, 1, 0) + jnp.where(z < nz - 1, 1, 0))

    pieces = tok // ROWS
    cuts = [pl.ds(q * ROWS, ROWS) for q in range(pieces)]

    def step_of(at, origin):
        reach = jnp.minimum(at, nz - 1 - at)
        gap = jnp.abs(origin - at)
        near = 2 * gap - jnp.where(origin < at, 1, 0)
        return jnp.clip(jnp.where(gap <= reach, near, gap + reach), 0, nz - 1)

    def piece(h, r, slot, q):
        return rows.at[h, slot, r, cuts[q]], row_sem.at[h, r, slot, q]

    def weights_of(r, slot):
        return grow.at[r, slot], g_sem.at[r, slot]

    for q in range(pieces):
        for step in (1, -1):
            valid = (z + step >= 0) & (z + step < nz)
            there = {"expert": (z + step) * 2 + c}
            slot = step_of(z + step, z)
            send(piece(0, 0, 0, q)[0], *piece(0, 0, slot, q), there, valid)
            if q == 0:
                send(grow.at[0, 0], *weights_of(0, slot), there, valid)
    for h in range(2):
        send(rows.at[h, 0, 0], rows.at[h, 0, 1], row_sem.at[h, 1, 0, 0], partner)
    send(grow.at[0, 0], *weights_of(1, 0), partner)
    for side in (1, 0):
        send(down_hbm.at[0, down_rows(1 - c, side), :], wd.at[1, side], w_sem.at[side], partner)

    def from_z(hop, q):
        for step in (1, -1):
            origin = z - step * hop
            valid = (origin >= 0) & (origin < nz)
            onward = valid & (z + step >= 0) & (z + step < nz)
            there = {"expert": (z + step) * 2 + c}
            slot, further = step_of(z, origin), step_of(z + step, origin)
            block, sem = piece(0, 0, slot, q)
            pl.when(valid)(functools.partial(arrived, block, sem))
            send(block, *piece(1, 0, slot, q), across, valid)
            if hop < nz - 1:
                send(block, *piece(0, 0, further, q), there, onward)
            send(block, *piece(0, 1, slot, q), partner, valid)
            if q == 0:
                line, sem = weights_of(0, slot)
                pl.when(valid)(functools.partial(arrived, line, sem))
                if hop < nz - 1:
                    send(line, *weights_of(0, further), there, onward)
                send(line, *weights_of(1, slot), partner, valid)

    def from_across(hop, q):
        for step in (1, -1):
            origin = z - step * hop
            valid = (origin >= 0) & (origin < nz)
            slot = step_of(z, origin)
            block, sem = piece(1, 0, slot, q)
            pl.when(valid)(functools.partial(arrived, block, sem))
            send(block, *piece(1, 1, slot, q), partner, valid)

    reach = jnp.minimum(z, nz - 1 - z)
    toward = jnp.where(2 * z < nz, 1, -1)

    def origin_of(s):
        if s == 0:
            return z
        near = z - (s + 1) // 2 * (1 if s % 2 else -1)
        return jnp.clip(jnp.where(s <= 2 * reach, near, z + toward * (s - reach)), 0, nz - 1)

    origins = [origin_of(s) for s in range(nz)]
    tile = 256 if units % 256 == 0 else LANES
    tiles = [pl.ds(t * tile, tile) for t in range(units // tile)]
    eye = lax.broadcasted_iota(jnp.int32, (tok, LANES), 0) == lax.broadcasted_iota(
        jnp.int32, (tok, LANES), 1
    )

    def ready(s, h):
        if s:
            for q in range(pieces):
                arrived(*piece(h, 1, s, q))
        else:
            arrived(rows.at[h, 0, 1], row_sem.at[h, 1, 0, 0])
        if h == 0:
            arrived(*weights_of(1, s))

    def product(first, count, h, weights, cols):
        return jnp.dot(
            rows[h, pl.ds(first, count)].reshape(count * both, half), weights[h, :, cols],
            preferred_element_type=f32,
        )

    def up_first_half(first, count):
        for s in range(first, first + count):
            ready(s, 0)
        for cols in tiles:
            early[0, : count * both, cols] = product(first, count, 0, wg, cols)
            early[1, : count * both, cols] = product(first, count, 0, wu, cols)

    def up(first, count, t):
        cols = tiles[t]
        at = pl.ds(first, count)

        scale = jnp.concatenate(
            [
                jnp.sum(jnp.where(eye, grow[r, s, me], 0.0), axis=1, keepdims=True)
                for s in range(first, first + count)
                for r in range(2)
            ],
            axis=0,
        )
        gate_act = early[0, : count * both, cols] + product(first, count, 1, wg, cols)
        up_act = early[1, : count * both, cols] + product(first, count, 1, wu, cols)
        value = gate_act / (1.0 + jnp.exp(-gate_act)) * up_act * scale
        value = value.astype(bf16).reshape(count, both, tile)
        hid[at, :, cols] = value
        hid_send[at, :tok, cols] = value[:, tok:]
        hid_send[at, tok:, cols] = value[:, :tok]

    def share(first, count):
        at = pl.ds(first, count)
        send(hid_send.at[at], hid_recv.at[at], h_sem.at[first], partner)

    def hidden(first, count):
        arrived(hid_recv.at[pl.ds(first, count)], h_sem.at[first])

    order = range(len(chunks))

    def down_product(source, which, first, count, side, cols):
        return lax.dot_general(
            source[pl.ds(first, count)].reshape(count * both, units), wd[which, side, cols, :],
            (((1,), (1,)), ((), ())), preferred_element_type=f32,
        )

    def down_own(first, count):
        for side in (1, 0):
            for n in order:
                cols = pl.ds(*chunks[n])
                ahead[side, : count * both, cols] = down_product(hid, 0, first, count, side, cols)

    def down(first, count, side, n):
        at, cols = pl.ds(first, count), pl.ds(*chunks[n])
        value = ahead[side, : count * both, cols] + down_product(
            hid_recv, 1, first, count, side, cols
        )
        value = value.reshape(count, both, chunks[n][1])
        if side == 0:
            keep[at, :, cols] = value
        else:
            b_send[at, :, cols] = value.astype(bf16)

    def release(s, n, when=None):
        cols = pl.ds(*chunks[n])
        send(b_send.at[s, :, cols], b_recv.at[s, :, cols], b_sem.at[s, n], across, when)

    def reduced(s, n, origin):
        cols = pl.ds(*chunks[n])
        arrived(b_recv.at[s, :, cols], b_sem.at[s, n])
        value = keep[s, :, cols] + b_recv[s, :, cols].astype(f32)
        if origin is None:
            keep[s, :, cols] = value
        else:
            c_send[s - 1, :, cols] = value.astype(bf16)
            send(
                c_send.at[s - 1, :, cols], c_recv.at[z, :, cols], c_sem.at[z, n],
                {"expert": origin * 2 + c},
            )

    def weights_of_down():
        for side in (1, 0):
            arrived(wd.at[1, side], w_sem.at[side])

    last = nz - 1
    waves = [(first, min(2, nz - first)) for first in range(0, nz, 2)]

    def begin(wave):
        first, count = waves[wave]
        if wave == 0:
            for copy in weight_copies:
                copy.wait()
        up_first_half(first, count)

    def gate_and_up(wave):
        first, count = waves[wave]
        for s in range(first, first + count):
            ready(s, 1)
        for t in range(len(tiles)):
            up(first, count, t)
        share(first, count)
        if wave == 0:
            for copy in down_copies:
                copy.wait()
        down_own(first, count)

    def own(s):
        return isinstance(s, int) and s == 0

    def turns(wave):
        first, count = waves[wave]
        if wave == 0 or count == 1:
            return [(s, origins[s]) for s in range(first + count - 1, first - 1, -1)]
        low = jnp.minimum(origins[first], origins[first + 1])
        high = jnp.maximum(origins[first], origins[first + 1])
        sooner = jnp.where(origins[first] < origins[first + 1], first, first + 1)
        return [(sooner, low), (2 * first + 1 - sooner, high)]

    def down_out(wave):
        first, count = waves[wave]
        hidden(first, count)
        if wave == 0:
            weights_of_down()
        for n in order:
            down(first, count, 1, n)
            release(turns(wave)[0][0], n)
        for s, _ in turns(wave)[1:]:
            for n in order:
                if not own(s):
                    release(s, n)
        if wave == 0:
            for n in order:
                release(0, n, z == 0)
        if wave == len(waves) - 1:
            for n in order:
                release(0, n, z > 0)

    def down_kept(wave):
        first, count = waves[wave]
        for n in order:
            down(first, count, 0, n)

    for q in range(pieces):
        from_z(1, q)
    for hop in range(2, last):
        for q in range(pieces):
            from_z(hop, q)
            from_across(hop - 1, q)
    if last > 1:
        from_z(last, 0)
        if last == 2:
            from_across(1, 0)
            for q in range(1, pieces):
                from_z(last, q)
                from_across(1, q)
            begin(0)
            gate_and_up(0)
        else:
            begin(0)
            gate_and_up(0)
            from_across(last - 1, 0)
            for q in range(1, pieces):
                from_z(last, q)
        down_out(0)
        if last > 2:
            for q in range(1, pieces):
                from_across(last - 1, q)
        down_kept(0)
        if len(waves) > 1:
            begin(1)
        for q in range(pieces):
            from_across(last, q)
    else:
        for q in range(pieces):
            from_across(1, q)
        begin(0)
        gate_and_up(0)
        down_out(0)
        down_kept(0)
    for wave in range(1, len(waves)):
        if wave > 1 or last < 2:
            begin(wave)
        gate_and_up(wave)
        older = len(pending)
        down_out(wave)
        for s, origin in turns(wave - 1):
            for n in order:
                if not own(s):
                    reduced(s, n, origin)
        down_kept(wave)
    for s, origin in turns(len(waves) - 1):
        for n in order:
            if not own(s):
                reduced(s, n, origin)
    if len(waves) > 1:
        drain(older)
    for n in order:
        reduced(0, n, None)

    base = c * half + x * quarter
    out_copies = []
    for n, (at, width) in enumerate(chunks):
        cols = pl.ds(at, width)
        value = keep[0, :, cols]
        for s in range(1, nz):
            slot = origins[s]
            arrived(c_recv.at[slot, :, cols], c_sem.at[slot, n])
            value = value + c_recv[slot, :, cols].astype(f32)
        d_send[:, cols] = value.astype(bf16)
        target = pl.ds(pl.multiple_of(base + at, LANES), width)
        near, far = d_send.at[:tok, cols], d_send.at[tok:, cols]
        send(far, out.at[:, target], d_sem.at[2, n], diagonal_peer)
        send(near, out.at[:, target], d_sem.at[0, n], across)
        send(far, out.at[:, target], d_sem.at[1, n], partner)
        out_copies.append(local(near, out.at[:, target]))

    for n, (at, width) in enumerate(chunks):
        for which, (core, side) in enumerate(((c, 1 - x), (1 - c, x), (1 - c, 1 - x))):
            start = pl.multiple_of(core * half + side * quarter + at, LANES)
            arrived(out.at[:, pl.ds(start, width)], d_sem.at[which, n])
    for copy in out_copies:
        copy.wait()
    drain(len(pending))


def fused_body(tokens, gates, slots, plan, gate_proj, up_proj, down_proj):
    f32, bf16 = jnp.float32, jnp.bfloat16
    nz = lax.axis_size("expert") // 2
    tok, model = tokens.shape
    top = gates.shape[1]
    half = model // 2
    quarter = half // 2
    units = gate_proj.shape[2]
    both = 2 * tok
    pieces = tok // ROWS
    chunks = split_tiles(quarter, CHUNKS)
    many = len(chunks)
    dma = pltpu.SemaphoreType.DMA
    anywhere = pl.BlockSpec(memory_space=pl.ANY)
    sends = 8 * nz * pieces + 4 * nz + 8 + nz + many * (2 * nz + 4)
    return pl.pallas_call(
        functools.partial(kernel, nz, chunks),
        out_shape=jax.ShapeDtypeStruct((tok, model), bf16),
        in_specs=[anywhere] * 7,
        out_specs=anywhere,
        scratch_shapes=[
            pltpu.VMEM((top, tok), f32),
            pltpu.VMEM((top, tok), jnp.int32),
            pltpu.SMEM(plan.shape, jnp.int32),
            pltpu.VMEM((2, nz, 2, tok, half), bf16),
            pltpu.VMEM((2, half, units), bf16),
            pltpu.VMEM((2, half, units), bf16),
            pltpu.VMEM((2, 2, quarter, units), bf16),
            pltpu.VMEM((nz, both, units), bf16),
            pltpu.VMEM((nz, both, units), bf16),
            pltpu.VMEM((nz, both, units), bf16),
            pltpu.VMEM((2, nz, 2 * nz, 1, LANES), f32),
            pltpu.VMEM((2, 2 * both, units), f32),
            pltpu.VMEM((2, 2 * both, quarter), f32),
            pltpu.VMEM((nz, both, quarter), f32),
            pltpu.VMEM((nz, both, quarter), bf16),
            pltpu.VMEM((nz, both, quarter), bf16),
            pltpu.VMEM((nz - 1, both, quarter), bf16),
            pltpu.VMEM((nz, both, quarter), bf16),
            pltpu.VMEM((both, quarter), bf16),
            dma((sends,)),
            dma((11 + many,)),
            dma((2, 2, nz, pieces)),
            dma((2, nz)),
            dma((2,)),
            dma((nz,)),
            dma((nz, many)),
            dma((nz, many)),
            dma((3, many)),
        ],
        compiler_params=pltpu.CompilerParams(
            collective_id=0, has_side_effects=True, vmem_limit_bytes=48 * 1024 * 1024
        ),
    )(*(pltpu.with_memory_space_constraint(a, pltpu.HBM) for a in (tokens, gates.T, slots.T, plan, gate_proj, up_proj, down_proj)))


def body(tokens, gates, slots, plan, gate_proj, up_proj, down_proj):
    experts, attn = lax.axis_size("expert"), lax.axis_size("attn")
    tok, model = tokens.shape
    fits = (
        attn == 2 and experts % 2 == 0 and experts > 2
        and tok % ROWS == 0 and tok <= LANES
        and model % (4 * LANES) == 0 and gate_proj.shape[0] == 1
        and gate_proj.shape[2] % LANES == 0
    )
    chosen = fused_body if fits else dense_body
    return chosen(tokens, gates, slots, plan, gate_proj, up_proj, down_proj)


def solution(mesh):
    return jax.shard_map(
        body,
        mesh=mesh,
        in_specs=(
            P(("groups", "expert"), None),
            P(("groups", "expert"), None),
            P(("groups", "expert"), None),
            P("groups"),
            P("expert", None, "attn"),
            P("expert", None, "attn"),
            P("expert", None, "attn"),
        ),
        out_specs=P(("groups", "expert"), None),
        check_vma=False,
    )
```

```python
import functools

import jax
import jax.numpy as jnp
from jax import lax
from jax.experimental import pallas as pl
from jax.experimental.pallas import tpu as pltpu
from jax.sharding import PartitionSpec as P

MESH = pl.DeviceIdType.MESH
LANES = 128
ROWS = 16
CHUNKS = 2


def combined_gates(gates, slots, plan, experts):
    choice = slots // 2
    expert = jnp.where(slots % 2 == 0, choice, plan[choice])
    ids = jnp.arange(experts, dtype=jnp.int32)
    return jnp.sum(jnp.where(expert[:, :, None] == ids, gates[:, :, None], 0.0), axis=1)


def dense_body(tokens, gates, slots, plan, gate_proj, up_proj, down_proj):
    experts = lax.axis_size("expert")
    weight = combined_gates(gates, slots, plan, experts)
    everyone = lax.all_gather(tokens, "expert", axis=0, tiled=True)
    weights = lax.all_to_all(weight, "expert", split_axis=1, concat_axis=0, tiled=True)
    gate_act = jnp.dot(everyone, gate_proj[0], preferred_element_type=jnp.float32)
    up_act = jnp.dot(everyone, up_proj[0], preferred_element_type=jnp.float32)
    hidden = (jax.nn.silu(gate_act) * up_act).astype(jnp.bfloat16)
    down = jnp.einsum("rf,df->rd", hidden, down_proj[0], preferred_element_type=jnp.float32)
    part = (down * weights).astype(jnp.bfloat16)
    part = lax.psum_scatter(part, "expert", scatter_dimension=0, tiled=True)
    return lax.psum(part, "attn")


def split_tiles(total, parts):
    tiles = total // LANES
    edges = [(tiles * p + parts - 1) // parts * LANES for p in range(parts + 1)]
    return [(a, b - a) for a, b in zip(edges, edges[1:]) if b > a]


def kernel(
    nz, chunks,
    tokens, gates_hbm, slots_hbm, plan_hbm, gate_hbm, up_hbm, down_hbm,
    out,
    gates, slots, plan, rows, wg, wu, wd, hid, hid_send, hid_recv, grow,
    early, ahead, keep, b_send, b_recv, c_send, c_recv, d_send,
    send_sem, local_sem, row_sem, g_sem, w_sem, h_sem, b_sem, c_sem, d_sem,
):
    f32, bf16 = jnp.float32, jnp.bfloat16
    experts = 2 * nz
    me = lax.axis_index("expert")
    x = lax.axis_index("attn")
    z, c = me // 2, me % 2
    tok, half = rows.shape[-2], rows.shape[-1]
    quarter = half // 2
    units = wg.shape[-1]
    both = 2 * tok
    mine = pl.ds(pl.multiple_of(x * half, LANES), half)
    other = pl.ds(pl.multiple_of((1 - x) * half, LANES), half)
    partner = {"expert": z * 2 + (1 - c)}
    across = {"attn": 1 - x}
    diagonal_peer = {"expert": z * 2 + (1 - c), "attn": 1 - x}

    barrier = pltpu.get_barrier_semaphore()

    def greet(peer):
        pl.semaphore_signal(barrier, inc=1, device_id=peer, device_id_type=MESH)

    greet(across)
    greet(partner)
    for step in (1, -1):
        pl.when((z + step >= 0) & (z + step < nz))(
            functools.partial(greet, {"expert": (z + step) * 2 + c})
        )

    counts = {"send": 0, "local": 0}
    pending = []

    def local(src, dst):
        copy = pltpu.make_async_copy(src, dst, local_sem.at[counts["local"]])
        counts["local"] += 1
        copy.start()
        return copy

    def prepare(src, dst, sem, device):
        copy = pltpu.make_async_remote_copy(
            src_ref=src, dst_ref=dst, send_sem=send_sem.at[counts["send"]], recv_sem=sem,
            device_id=device, device_id_type=MESH,
        )
        counts["send"] += 1
        return copy

    def send(src, dst, sem, device, when=None):
        copy = prepare(src, dst, sem, device)
        if when is None:
            copy.start()
        else:
            pl.when(when)(copy.start)
        pending.append((when, copy))

    def drain(count):
        for _ in range(count):
            when, copy = pending.pop(0)
            if when is None:
                copy.wait_send()
            else:
                pl.when(when)(copy.wait_send)

    def arrived(dst, sem):
        pltpu.make_async_remote_copy(
            src_ref=dst, dst_ref=dst, send_sem=send_sem.at[0], recv_sem=sem,
            device_id=partner, device_id_type=MESH,
        ).wait_recv()

    own_copies = [
        local(tokens.at[:, mine], rows.at[0, 0, 0]),
        local(tokens.at[:, other], rows.at[1, 0, 0]),
    ]
    small_copies = [local(gates_hbm, gates), local(slots_hbm, slots), local(plan_hbm, plan)]
    weight_copies = []
    for h, part in enumerate((mine, other)):
        weight_copies.append(local(gate_hbm.at[0, part, :], wg.at[h]))
        weight_copies.append(local(up_hbm.at[0, part, :], wu.at[h]))

    def down_rows(core, side):
        start = core * half + (x if side == 0 else 1 - x) * quarter
        return pl.ds(pl.multiple_of(start, LANES), quarter)

    down_copies = [
        local(down_hbm.at[0, down_rows(c, side), :], wd.at[0, side]) for side in (1, 0)
    ]

    for copy in small_copies:
        copy.wait()
    named = slots[...]
    expert = lax.shift_right_logical(named, 1)
    target = expert
    for d in range(experts):
        target = jnp.where(expert == d, plan[d], target)
    expert = jnp.where((named & 1) == 0, expert, target)
    gate = gates[...]
    for e in range(experts):
        grow[0, 0, e, :, :tok] = jnp.sum(jnp.where(expert == e, gate, 0.0), axis=0, keepdims=True)
    for copy in own_copies:
        copy.wait()

    pl.semaphore_wait(barrier, 2 + jnp.where(z > 0, 1, 0) + jnp.where(z < nz - 1, 1, 0))

    pieces = tok // ROWS
    cuts = [pl.ds(q * ROWS, ROWS) for q in range(pieces)]

    def step_of(at, origin):
        reach = jnp.minimum(at, nz - 1 - at)
        gap = jnp.abs(origin - at)
        near = 2 * gap - jnp.where(origin < at, 1, 0)
        return jnp.clip(jnp.where(gap <= reach, near, gap + reach), 0, nz - 1)

    def piece(h, r, slot, q):
        return rows.at[h, slot, r, cuts[q]], row_sem.at[h, r, slot, q]

    def weights_of(r, slot):
        return grow.at[r, slot], g_sem.at[r, slot]

    for q in range(pieces):
        for step in (1, -1):
            valid = (z + step >= 0) & (z + step < nz)
            there = {"expert": (z + step) * 2 + c}
            slot = step_of(z + step, z)
            send(piece(0, 0, 0, q)[0], *piece(0, 0, slot, q), there, valid)
            if q == 0:
                send(grow.at[0, 0], *weights_of(0, slot), there, valid)
    for h in range(2):
        send(rows.at[h, 0, 0], rows.at[h, 0, 1], row_sem.at[h, 1, 0, 0], partner)
    send(grow.at[0, 0], *weights_of(1, 0), partner)
    for side in (1, 0):
        send(down_hbm.at[0, down_rows(1 - c, side), :], wd.at[1, side], w_sem.at[side], partner)

    def from_z(hop, q):
        for step in (1, -1):
            origin = z - step * hop
            valid = (origin >= 0) & (origin < nz)
            onward = valid & (z + step >= 0) & (z + step < nz)
            there = {"expert": (z + step) * 2 + c}
            slot, further = step_of(z, origin), step_of(z + step, origin)
            block, sem = piece(0, 0, slot, q)
            pl.when(valid)(functools.partial(arrived, block, sem))
            send(block, *piece(1, 0, slot, q), across, valid)
            if hop < nz - 1:
                send(block, *piece(0, 0, further, q), there, onward)
            send(block, *piece(0, 1, slot, q), partner, valid)
            if q == 0:
                line, sem = weights_of(0, slot)
                pl.when(valid)(functools.partial(arrived, line, sem))
                if hop < nz - 1:
                    send(line, *weights_of(0, further), there, onward)
                send(line, *weights_of(1, slot), partner, valid)

    def from_across(hop, q):
        for step in (1, -1):
            origin = z - step * hop
            valid = (origin >= 0) & (origin < nz)
            slot = step_of(z, origin)
            block, sem = piece(1, 0, slot, q)
            pl.when(valid)(functools.partial(arrived, block, sem))
            send(block, *piece(1, 1, slot, q), partner, valid)

    reach = jnp.minimum(z, nz - 1 - z)
    toward = jnp.where(2 * z < nz, 1, -1)

    def origin_of(s):
        if s == 0:
            return z
        near = z - (s + 1) // 2 * (1 if s % 2 else -1)
        return jnp.clip(jnp.where(s <= 2 * reach, near, z + toward * (s - reach)), 0, nz - 1)

    origins = [origin_of(s) for s in range(nz)]
    tile = 256 if units % 256 == 0 else LANES
    tiles = [pl.ds(t * tile, tile) for t in range(units // tile)]
    eye = lax.broadcasted_iota(jnp.int32, (tok, LANES), 0) == lax.broadcasted_iota(
        jnp.int32, (tok, LANES), 1
    )

    def ready(s, h):
        if s:
            for q in range(pieces):
                arrived(*piece(h, 1, s, q))
        else:
            arrived(rows.at[h, 0, 1], row_sem.at[h, 1, 0, 0])
        if h == 0:
            arrived(*weights_of(1, s))

    def product(first, count, h, weights, cols):
        return jnp.dot(
            rows[h, pl.ds(first, count)].reshape(count * both, half), weights[h, :, cols],
            preferred_element_type=f32,
        )

    def up_first_half(first, count):
        for s in range(first, first + count):
            ready(s, 0)
        for cols in tiles:
            early[0, : count * both, cols] = product(first, count, 0, wg, cols)
            early[1, : count * both, cols] = product(first, count, 0, wu, cols)

    def up(first, count, t):
        cols = tiles[t]
        at = pl.ds(first, count)

        scale = jnp.concatenate(
            [
                jnp.sum(jnp.where(eye, grow[r, s, me], 0.0), axis=1, keepdims=True)
                for s in range(first, first + count)
                for r in range(2)
            ],
            axis=0,
        )
        gate_act = early[0, : count * both, cols] + product(first, count, 1, wg, cols)
        up_act = early[1, : count * both, cols] + product(first, count, 1, wu, cols)
        value = gate_act / (1.0 + jnp.exp(-gate_act)) * up_act * scale
        value = value.astype(bf16).reshape(count, both, tile)
        hid[at, :, cols] = value
        hid_send[at, :tok, cols] = value[:, tok:]
        hid_send[at, tok:, cols] = value[:, :tok]

    def share(first, count):
        at = pl.ds(first, count)
        send(hid_send.at[at], hid_recv.at[at], h_sem.at[first], partner)

    def hidden(first, count):
        arrived(hid_recv.at[pl.ds(first, count)], h_sem.at[first])

    order = range(len(chunks))

    def down_product(source, which, first, count, side, cols):
        return lax.dot_general(
            source[pl.ds(first, count)].reshape(count * both, units), wd[which, side, cols, :],
            (((1,), (1,)), ((), ())), preferred_element_type=f32,
        )

    def down_own(first, count):
        for side in (1, 0):
            for n in order:
                cols = pl.ds(*chunks[n])
                ahead[side, : count * both, cols] = down_product(hid, 0, first, count, side, cols)

    def down(first, count, side, n):
        at, cols = pl.ds(first, count), pl.ds(*chunks[n])
        value = ahead[side, : count * both, cols] + down_product(
            hid_recv, 1, first, count, side, cols
        )
        value = value.reshape(count, both, chunks[n][1])
        if side == 0:
            keep[at, :, cols] = value
        else:
            b_send[at, :, cols] = value.astype(bf16)

    def release(s, n, when=None):
        cols = pl.ds(*chunks[n])
        send(b_send.at[s, :, cols], b_recv.at[s, :, cols], b_sem.at[s, n], across, when)

    def reduced(s, n, origin):
        cols = pl.ds(*chunks[n])
        arrived(b_recv.at[s, :, cols], b_sem.at[s, n])
        value = keep[s, :, cols] + b_recv[s, :, cols].astype(f32)
        if origin is None:
            keep[s, :, cols] = value
        else:
            c_send[s - 1, :, cols] = value.astype(bf16)
            send(
                c_send.at[s - 1, :, cols], c_recv.at[z, :, cols], c_sem.at[z, n],
                {"expert": origin * 2 + c},
            )

    def weights_of_down():
        for side in (1, 0):
            arrived(wd.at[1, side], w_sem.at[side])

    last = nz - 1
    waves = [(first, min(2, nz - first)) for first in range(0, nz, 2)]

    def begin(wave):
        first, count = waves[wave]
        if wave == 0:
            for copy in weight_copies:
                copy.wait()
        up_first_half(first, count)

    def gate_and_up(wave):
        first, count = waves[wave]
        for s in range(first, first + count):
            ready(s, 1)
        for t in range(len(tiles)):
            up(first, count, t)
        share(first, count)
        if wave == 0:
            for copy in down_copies:
                copy.wait()
        down_own(first, count)

    def own(s):
        return isinstance(s, int) and s == 0

    def turns(wave):
        first, count = waves[wave]
        if wave == 0 or count == 1:
            return [(s, origins[s]) for s in range(first + count - 1, first - 1, -1)]
        low = jnp.minimum(origins[first], origins[first + 1])
        high = jnp.maximum(origins[first], origins[first + 1])
        sooner = jnp.where(origins[first] < origins[first + 1], first, first + 1)
        return [(sooner, low), (2 * first + 1 - sooner, high)]

    def down_out(wave):
        first, count = waves[wave]
        hidden(first, count)
        if wave == 0:
            weights_of_down()
        for n in order:
            down(first, count, 1, n)
            release(turns(wave)[0][0], n)
        for s, _ in turns(wave)[1:]:
            for n in order:
                if not own(s):
                    release(s, n)
        if wave == 0:
            for n in order:
                release(0, n, z == 0)
        if wave == len(waves) - 1:
            for n in order:
                release(0, n, z > 0)

    def down_kept(wave):
        first, count = waves[wave]
        for n in order:
            down(first, count, 0, n)

    for q in range(pieces):
        from_z(1, q)
    for hop in range(2, last):
        for q in range(pieces):
            from_z(hop, q)
            from_across(hop - 1, q)
    if last > 1:
        from_z(last, 0)
        if last == 2:
            from_across(1, 0)
            for q in range(1, pieces):
                from_z(last, q)
                from_across(1, q)
            begin(0)
            gate_and_up(0)
        else:
            begin(0)
            gate_and_up(0)
            from_across(last - 1, 0)
            for q in range(1, pieces):
                from_z(last, q)
        if last > 2:
            for q in range(1, pieces):
                from_across(last - 1, q)
        down_out(0)
        down_kept(0)
        if len(waves) > 1:
            begin(1)
        for q in range(pieces):
            from_across(last, q)
    else:
        for q in range(pieces):
            from_across(1, q)
        begin(0)
        gate_and_up(0)
        down_out(0)
        down_kept(0)
    for wave in range(1, len(waves)):
        if wave > 1 or last < 2:
            begin(wave)
        gate_and_up(wave)
        older = len(pending)
        down_out(wave)
        for s, origin in turns(wave - 1):
            for n in order:
                if not own(s):
                    reduced(s, n, origin)
        down_kept(wave)
    for s, origin in turns(len(waves) - 1):
        for n in order:
            if not own(s):
                reduced(s, n, origin)
    if len(waves) > 1:
        drain(older)
    for n in order:
        reduced(0, n, None)

    base = c * half + x * quarter
    out_copies = []
    for n, (at, width) in enumerate(chunks):
        cols = pl.ds(at, width)
        value = keep[0, :, cols]
        for s in range(1, nz):
            slot = origins[s]
            arrived(c_recv.at[slot, :, cols], c_sem.at[slot, n])
            value = value + c_recv[slot, :, cols].astype(f32)
        d_send[:, cols] = value.astype(bf16)
        target = pl.ds(pl.multiple_of(base + at, LANES), width)
        near, far = d_send.at[:tok, cols], d_send.at[tok:, cols]
        send(far, out.at[:, target], d_sem.at[2, n], diagonal_peer)
        send(near, out.at[:, target], d_sem.at[0, n], across)
        send(far, out.at[:, target], d_sem.at[1, n], partner)
        out_copies.append(local(near, out.at[:, target]))

    for n, (at, width) in enumerate(chunks):
        for which, (core, side) in enumerate(((c, 1 - x), (1 - c, x), (1 - c, 1 - x))):
            start = pl.multiple_of(core * half + side * quarter + at, LANES)
            arrived(out.at[:, pl.ds(start, width)], d_sem.at[which, n])
    for copy in out_copies:
        copy.wait()
    drain(len(pending))


def fused_body(tokens, gates, slots, plan, gate_proj, up_proj, down_proj):
    f32, bf16 = jnp.float32, jnp.bfloat16
    nz = lax.axis_size("expert") // 2
    tok, model = tokens.shape
    top = gates.shape[1]
    half = model // 2
    quarter = half // 2
    units = gate_proj.shape[2]
    both = 2 * tok
    pieces = tok // ROWS
    chunks = split_tiles(quarter, CHUNKS)
    many = len(chunks)
    dma = pltpu.SemaphoreType.DMA
    anywhere = pl.BlockSpec(memory_space=pl.ANY)
    sends = 8 * nz * pieces + 4 * nz + 8 + nz + many * (2 * nz + 4)
    return pl.pallas_call(
        functools.partial(kernel, nz, chunks),
        out_shape=jax.ShapeDtypeStruct((tok, model), bf16),
        in_specs=[anywhere] * 7,
        out_specs=anywhere,
        scratch_shapes=[
            pltpu.VMEM((top, tok), f32),
            pltpu.VMEM((top, tok), jnp.int32),
            pltpu.SMEM(plan.shape, jnp.int32),
            pltpu.VMEM((2, nz, 2, tok, half), bf16),
            pltpu.VMEM((2, half, units), bf16),
            pltpu.VMEM((2, half, units), bf16),
            pltpu.VMEM((2, 2, quarter, units), bf16),
            pltpu.VMEM((nz, both, units), bf16),
            pltpu.VMEM((nz, both, units), bf16),
            pltpu.VMEM((nz, both, units), bf16),
            pltpu.VMEM((2, nz, 2 * nz, 1, LANES), f32),
            pltpu.VMEM((2, 2 * both, units), f32),
            pltpu.VMEM((2, 2 * both, quarter), f32),
            pltpu.VMEM((nz, both, quarter), f32),
            pltpu.VMEM((nz, both, quarter), bf16),
            pltpu.VMEM((nz, both, quarter), bf16),
            pltpu.VMEM((nz - 1, both, quarter), bf16),
            pltpu.VMEM((nz, both, quarter), bf16),
            pltpu.VMEM((both, quarter), bf16),
            dma((sends,)),
            dma((11 + many,)),
            dma((2, 2, nz, pieces)),
            dma((2, nz)),
            dma((2,)),
            dma((nz,)),
            dma((nz, many)),
            dma((nz, many)),
            dma((3, many)),
        ],
        compiler_params=pltpu.CompilerParams(
            collective_id=0, has_side_effects=True, vmem_limit_bytes=48 * 1024 * 1024
        ),
    )(*(pltpu.with_memory_space_constraint(a, pltpu.HBM) for a in (tokens, gates.T, slots.T, plan, gate_proj, up_proj, down_proj)))


def body(tokens, gates, slots, plan, gate_proj, up_proj, down_proj):
    experts, attn = lax.axis_size("expert"), lax.axis_size("attn")
    tok, model = tokens.shape
    fits = (
        attn == 2 and experts % 2 == 0 and experts > 2
        and tok % ROWS == 0 and tok <= LANES
        and model % (4 * LANES) == 0 and gate_proj.shape[0] == 1
        and gate_proj.shape[2] % LANES == 0
    )
    chosen = fused_body if fits else dense_body
    return chosen(tokens, gates, slots, plan, gate_proj, up_proj, down_proj)


def solution(mesh):
    return jax.shard_map(
        body,
        mesh=mesh,
        in_specs=(
            P(("groups", "expert"), None),
            P(("groups", "expert"), None),
            P(("groups", "expert"), None),
            P("groups"),
            P("expert", None, "attn"),
            P("expert", None, "attn"),
            P("expert", None, "attn"),
        ),
        out_specs=P(("groups", "expert"), None),
        check_vma=False,
    )
```

```python
import functools

import jax
import jax.numpy as jnp
from jax import lax
from jax.experimental import pallas as pl
from jax.experimental.pallas import tpu as pltpu
from jax.sharding import PartitionSpec as P

MESH = pl.DeviceIdType.MESH
LANES = 128
ROWS = 16
CHUNKS = 2


def combined_gates(gates, slots, plan, experts):
    choice = slots // 2
    expert = jnp.where(slots % 2 == 0, choice, plan[choice])
    ids = jnp.arange(experts, dtype=jnp.int32)
    return jnp.sum(jnp.where(expert[:, :, None] == ids, gates[:, :, None], 0.0), axis=1)


def dense_body(tokens, gates, slots, plan, gate_proj, up_proj, down_proj):
    experts = lax.axis_size("expert")
    weight = combined_gates(gates, slots, plan, experts)
    everyone = lax.all_gather(tokens, "expert", axis=0, tiled=True)
    weights = lax.all_to_all(weight, "expert", split_axis=1, concat_axis=0, tiled=True)
    gate_act = jnp.dot(everyone, gate_proj[0], preferred_element_type=jnp.float32)
    up_act = jnp.dot(everyone, up_proj[0], preferred_element_type=jnp.float32)
    hidden = (jax.nn.silu(gate_act) * up_act).astype(jnp.bfloat16)
    down = jnp.einsum("rf,df->rd", hidden, down_proj[0], preferred_element_type=jnp.float32)
    part = (down * weights).astype(jnp.bfloat16)
    part = lax.psum_scatter(part, "expert", scatter_dimension=0, tiled=True)
    return lax.psum(part, "attn")


def split_tiles(total, parts):
    tiles = total // LANES
    edges = [(tiles * p + parts - 1) // parts * LANES for p in range(parts + 1)]
    return [(a, b - a) for a, b in zip(edges, edges[1:]) if b > a]


def kernel(
    nz, chunks,
    tokens, gates_hbm, slots_hbm, plan_hbm, gate_hbm, up_hbm, down_hbm,
    out,
    gates, slots, plan, rows, wg, wu, wd, hid, hid_send, hid_recv, grow,
    early, ahead, keep, b_send, b_recv, c_send, c_recv, d_send,
    send_sem, local_sem, row_sem, g_sem, w_sem, h_sem, b_sem, c_sem, d_sem,
):
    f32, bf16 = jnp.float32, jnp.bfloat16
    experts = 2 * nz
    me = lax.axis_index("expert")
    x = lax.axis_index("attn")
    z, c = me // 2, me % 2
    tok, half = rows.shape[-2], rows.shape[-1]
    quarter = half // 2
    units = wg.shape[-1]
    both = 2 * tok
    mine = pl.ds(pl.multiple_of(x * half, LANES), half)
    other = pl.ds(pl.multiple_of((1 - x) * half, LANES), half)
    partner = {"expert": z * 2 + (1 - c)}
    across = {"attn": 1 - x}
    diagonal_peer = {"expert": z * 2 + (1 - c), "attn": 1 - x}

    barrier = pltpu.get_barrier_semaphore()

    def greet(peer):
        pl.semaphore_signal(barrier, inc=1, device_id=peer, device_id_type=MESH)

    greet(across)
    greet(partner)
    for step in (1, -1):
        pl.when((z + step >= 0) & (z + step < nz))(
            functools.partial(greet, {"expert": (z + step) * 2 + c})
        )

    counts = {"send": 0, "local": 0}
    pending = []

    def local(src, dst):
        copy = pltpu.make_async_copy(src, dst, local_sem.at[counts["local"]])
        counts["local"] += 1
        copy.start()
        return copy

    def prepare(src, dst, sem, device):
        copy = pltpu.make_async_remote_copy(
            src_ref=src, dst_ref=dst, send_sem=send_sem.at[counts["send"]], recv_sem=sem,
            device_id=device, device_id_type=MESH,
        )
        counts["send"] += 1
        return copy

    def send(src, dst, sem, device, when=None):
        copy = prepare(src, dst, sem, device)
        if when is None:
            copy.start()
        else:
            pl.when(when)(copy.start)
        pending.append((when, copy))

    def drain(count):
        for _ in range(count):
            when, copy = pending.pop(0)
            if when is None:
                copy.wait_send()
            else:
                pl.when(when)(copy.wait_send)

    def arrived(dst, sem):
        pltpu.make_async_remote_copy(
            src_ref=dst, dst_ref=dst, send_sem=send_sem.at[0], recv_sem=sem,
            device_id=partner, device_id_type=MESH,
        ).wait_recv()

    own_copies = [
        local(tokens.at[:, mine], rows.at[0, 0, 0]),
        local(tokens.at[:, other], rows.at[1, 0, 0]),
    ]
    small_copies = [local(gates_hbm, gates), local(slots_hbm, slots), local(plan_hbm, plan)]
    weight_copies = []
    for h, part in enumerate((mine, other)):
        weight_copies.append(local(gate_hbm.at[0, part, :], wg.at[h]))
        weight_copies.append(local(up_hbm.at[0, part, :], wu.at[h]))

    def down_rows(core, side):
        start = core * half + (x if side == 0 else 1 - x) * quarter
        return pl.ds(pl.multiple_of(start, LANES), quarter)

    down_copies = [
        local(down_hbm.at[0, down_rows(c, side), :], wd.at[0, side]) for side in (1, 0)
    ]

    for copy in small_copies:
        copy.wait()
    named = slots[...]
    expert = lax.shift_right_logical(named, 1)
    target = expert
    for d in range(experts):
        target = jnp.where(expert == d, plan[d], target)
    expert = jnp.where((named & 1) == 0, expert, target)
    gate = gates[...]
    for e in range(experts):
        grow[0, 0, e, :, :tok] = jnp.sum(jnp.where(expert == e, gate, 0.0), axis=0, keepdims=True)
    for copy in own_copies:
        copy.wait()

    pl.semaphore_wait(barrier, 2 + jnp.where(z > 0, 1, 0) + jnp.where(z < nz - 1, 1, 0))

    pieces = tok // ROWS
    cuts = [pl.ds(q * ROWS, ROWS) for q in range(pieces)]

    def step_of(at, origin):
        reach = jnp.minimum(at, nz - 1 - at)
        gap = jnp.abs(origin - at)
        near = 2 * gap - jnp.where(origin < at, 1, 0)
        return jnp.clip(jnp.where(gap <= reach, near, gap + reach), 0, nz - 1)

    def piece(h, r, slot, q):
        return rows.at[h, slot, r, cuts[q]], row_sem.at[h, r, slot, q]

    def weights_of(r, slot):
        return grow.at[r, slot], g_sem.at[r, slot]

    for q in range(pieces):
        for step in (1, -1):
            valid = (z + step >= 0) & (z + step < nz)
            there = {"expert": (z + step) * 2 + c}
            slot = step_of(z + step, z)
            send(piece(0, 0, 0, q)[0], *piece(0, 0, slot, q), there, valid)
            if q == 0:
                send(grow.at[0, 0], *weights_of(0, slot), there, valid)
    for h in range(2):
        send(rows.at[h, 0, 0], rows.at[h, 0, 1], row_sem.at[h, 1, 0, 0], partner)
    send(grow.at[0, 0], *weights_of(1, 0), partner)
    for side in (1, 0):
        send(down_hbm.at[0, down_rows(1 - c, side), :], wd.at[1, side], w_sem.at[side], partner)

    def from_z(hop, q):
        for step in (1, -1):
            origin = z - step * hop
            valid = (origin >= 0) & (origin < nz)
            onward = valid & (z + step >= 0) & (z + step < nz)
            there = {"expert": (z + step) * 2 + c}
            slot, further = step_of(z, origin), step_of(z + step, origin)
            block, sem = piece(0, 0, slot, q)
            pl.when(valid)(functools.partial(arrived, block, sem))
            if hop < nz - 1:
                send(block, *piece(0, 0, further, q), there, onward)
            send(block, *piece(1, 0, slot, q), across, valid)
            send(block, *piece(0, 1, slot, q), partner, valid)
            if q == 0:
                line, sem = weights_of(0, slot)
                pl.when(valid)(functools.partial(arrived, line, sem))
                if hop < nz - 1:
                    send(line, *weights_of(0, further), there, onward)
                send(line, *weights_of(1, slot), partner, valid)

    def from_across(hop, q):
        for step in (1, -1):
            origin = z - step * hop
            valid = (origin >= 0) & (origin < nz)
            slot = step_of(z, origin)
            block, sem = piece(1, 0, slot, q)
            pl.when(valid)(functools.partial(arrived, block, sem))
            send(block, *piece(1, 1, slot, q), partner, valid)

    reach = jnp.minimum(z, nz - 1 - z)
    toward = jnp.where(2 * z < nz, 1, -1)

    def origin_of(s):
        if s == 0:
            return z
        near = z - (s + 1) // 2 * (1 if s % 2 else -1)
        return jnp.clip(jnp.where(s <= 2 * reach, near, z + toward * (s - reach)), 0, nz - 1)

    origins = [origin_of(s) for s in range(nz)]
    tile = 256 if units % 256 == 0 else LANES
    tiles = [pl.ds(t * tile, tile) for t in range(units // tile)]
    eye = lax.broadcasted_iota(jnp.int32, (tok, LANES), 0) == lax.broadcasted_iota(
        jnp.int32, (tok, LANES), 1
    )

    def ready(s, h):
        if s:
            for q in range(pieces):
                arrived(*piece(h, 1, s, q))
        else:
            arrived(rows.at[h, 0, 1], row_sem.at[h, 1, 0, 0])
        if h == 0:
            arrived(*weights_of(1, s))

    def product(first, count, h, weights, cols):
        return jnp.dot(
            rows[h, pl.ds(first, count)].reshape(count * both, half), weights[h, :, cols],
            preferred_element_type=f32,
        )

    def up_first_half(first, count):
        for s in range(first, first + count):
            ready(s, 0)
        for cols in tiles:
            early[0, : count * both, cols] = product(first, count, 0, wg, cols)
            early[1, : count * both, cols] = product(first, count, 0, wu, cols)

    def up(first, count, t):
        cols = tiles[t]
        at = pl.ds(first, count)

        scale = jnp.concatenate(
            [
                jnp.sum(jnp.where(eye, grow[r, s, me], 0.0), axis=1, keepdims=True)
                for s in range(first, first + count)
                for r in range(2)
            ],
            axis=0,
        )
        gate_act = early[0, : count * both, cols] + product(first, count, 1, wg, cols)
        up_act = early[1, : count * both, cols] + product(first, count, 1, wu, cols)
        value = gate_act / (1.0 + jnp.exp(-gate_act)) * up_act * scale
        value = value.astype(bf16).reshape(count, both, tile)
        hid[at, :, cols] = value
        hid_send[at, :tok, cols] = value[:, tok:]
        hid_send[at, tok:, cols] = value[:, :tok]

    def share(first, count):
        at = pl.ds(first, count)
        send(hid_send.at[at], hid_recv.at[at], h_sem.at[first], partner)

    def hidden(first, count):
        arrived(hid_recv.at[pl.ds(first, count)], h_sem.at[first])

    order = range(len(chunks))

    def down_product(source, which, first, count, side, cols):
        return lax.dot_general(
            source[pl.ds(first, count)].reshape(count * both, units), wd[which, side, cols, :],
            (((1,), (1,)), ((), ())), preferred_element_type=f32,
        )

    def down_own(first, count):
        for side in (1, 0):
            for n in order:
                cols = pl.ds(*chunks[n])
                ahead[side, : count * both, cols] = down_product(hid, 0, first, count, side, cols)

    def down(first, count, side, n):
        at, cols = pl.ds(first, count), pl.ds(*chunks[n])
        value = ahead[side, : count * both, cols] + down_product(
            hid_recv, 1, first, count, side, cols
        )
        value = value.reshape(count, both, chunks[n][1])
        if side == 0:
            keep[at, :, cols] = value
        else:
            b_send[at, :, cols] = value.astype(bf16)

    def release(s, n, when=None):
        cols = pl.ds(*chunks[n])
        send(b_send.at[s, :, cols], b_recv.at[s, :, cols], b_sem.at[s, n], across, when)

    def reduced(s, n, origin):
        cols = pl.ds(*chunks[n])
        arrived(b_recv.at[s, :, cols], b_sem.at[s, n])
        value = keep[s, :, cols] + b_recv[s, :, cols].astype(f32)
        if origin is None:
            keep[s, :, cols] = value
        else:
            c_send[s - 1, :, cols] = value.astype(bf16)
            send(
                c_send.at[s - 1, :, cols], c_recv.at[z, :, cols], c_sem.at[z, n],
                {"expert": origin * 2 + c},
            )

    def weights_of_down():
        for side in (1, 0):
            arrived(wd.at[1, side], w_sem.at[side])

    last = nz - 1
    waves = [(first, min(2, nz - first)) for first in range(0, nz, 2)]

    def begin(wave):
        first, count = waves[wave]
        if wave == 0:
            for copy in weight_copies:
                copy.wait()
        up_first_half(first, count)

    def gate_and_up(wave):
        first, count = waves[wave]
        for s in range(first, first + count):
            ready(s, 1)
        for t in range(len(tiles)):
            up(first, count, t)
        share(first, count)
        if wave == 0:
            for copy in down_copies:
                copy.wait()
        down_own(first, count)

    def own(s):
        return isinstance(s, int) and s == 0

    def turns(wave):
        first, count = waves[wave]
        if wave == 0 or count == 1:
            return [(s, origins[s]) for s in range(first + count - 1, first - 1, -1)]
        low = jnp.minimum(origins[first], origins[first + 1])
        high = jnp.maximum(origins[first], origins[first + 1])
        sooner = jnp.where(origins[first] < origins[first + 1], first, first + 1)
        return [(sooner, low), (2 * first + 1 - sooner, high)]

    def down_out(wave):
        first, count = waves[wave]
        hidden(first, count)
        if wave == 0:
            weights_of_down()
        for n in order:
            down(first, count, 1, n)
            release(turns(wave)[0][0], n)
        for s, _ in turns(wave)[1:]:
            for n in order:
                if not own(s):
                    release(s, n)
        if wave == 0:
            for n in order:
                release(0, n, z == 0)
        if wave == len(waves) - 1:
            for n in order:
                release(0, n, z > 0)

    def down_kept(wave):
        first, count = waves[wave]
        for n in order:
            down(first, count, 0, n)

    for q in range(pieces):
        from_z(1, q)
    for hop in range(2, last):
        for q in range(pieces):
            from_z(hop, q)
            from_across(hop - 1, q)
    if last > 1:
        from_z(last, 0)
        if last == 2:
            from_across(1, 0)
            for q in range(1, pieces):
                from_z(last, q)
                from_across(1, q)
            begin(0)
            gate_and_up(0)
        else:
            begin(0)
            gate_and_up(0)
            from_across(last - 1, 0)
            for q in range(1, pieces):
                from_z(last, q)
        if last > 2:
            for q in range(1, pieces):
                from_across(last - 1, q)
        down_out(0)
        from_across(last, 0)
        if len(waves) > 1:
            begin(1)
        for q in range(1, pieces):
            from_across(last, q)
        down_kept(0)
    else:
        for q in range(pieces):
            from_across(1, q)
        begin(0)
        gate_and_up(0)
        down_out(0)
        down_kept(0)
    for wave in range(1, len(waves)):
        if wave > 1 or last < 2:
            begin(wave)
        gate_and_up(wave)
        older = len(pending)
        down_out(wave)
        for s, origin in turns(wave - 1):
            for n in order:
                if not own(s):
                    reduced(s, n, origin)
        down_kept(wave)
    for s, origin in turns(len(waves) - 1):
        for n in order:
            if not own(s):
                reduced(s, n, origin)
    if len(waves) > 1:
        drain(older)
    for n in order:
        reduced(0, n, None)

    base = c * half + x * quarter
    out_copies = []
    for n, (at, width) in enumerate(chunks):
        cols = pl.ds(at, width)
        value = keep[0, :, cols]
        for s in range(1, nz):
            slot = origins[s]
            arrived(c_recv.at[slot, :, cols], c_sem.at[slot, n])
            value = value + c_recv[slot, :, cols].astype(f32)
        d_send[:, cols] = value.astype(bf16)
        target = pl.ds(pl.multiple_of(base + at, LANES), width)
        near, far = d_send.at[:tok, cols], d_send.at[tok:, cols]
        send(far, out.at[:, target], d_sem.at[2, n], diagonal_peer)
        send(near, out.at[:, target], d_sem.at[0, n], across)
        send(far, out.at[:, target], d_sem.at[1, n], partner)
        out_copies.append(local(near, out.at[:, target]))

    for n, (at, width) in enumerate(chunks):
        for which, (core, side) in enumerate(((c, 1 - x), (1 - c, x), (1 - c, 1 - x))):
            start = pl.multiple_of(core * half + side * quarter + at, LANES)
            arrived(out.at[:, pl.ds(start, width)], d_sem.at[which, n])
    for copy in out_copies:
        copy.wait()
    drain(len(pending))


def fused_body(tokens, gates, slots, plan, gate_proj, up_proj, down_proj):
    f32, bf16 = jnp.float32, jnp.bfloat16
    nz = lax.axis_size("expert") // 2
    tok, model = tokens.shape
    top = gates.shape[1]
    half = model // 2
    quarter = half // 2
    units = gate_proj.shape[2]
    both = 2 * tok
    pieces = tok // ROWS
    chunks = split_tiles(quarter, CHUNKS)
    many = len(chunks)
    dma = pltpu.SemaphoreType.DMA
    anywhere = pl.BlockSpec(memory_space=pl.ANY)
    sends = 8 * nz * pieces + 4 * nz + 8 + nz + many * (2 * nz + 4)
    return pl.pallas_call(
        functools.partial(kernel, nz, chunks),
        out_shape=jax.ShapeDtypeStruct((tok, model), bf16),
        in_specs=[anywhere] * 7,
        out_specs=anywhere,
        scratch_shapes=[
            pltpu.VMEM((top, tok), f32),
            pltpu.VMEM((top, tok), jnp.int32),
            pltpu.SMEM(plan.shape, jnp.int32),
            pltpu.VMEM((2, nz, 2, tok, half), bf16),
            pltpu.VMEM((2, half, units), bf16),
            pltpu.VMEM((2, half, units), bf16),
            pltpu.VMEM((2, 2, quarter, units), bf16),
            pltpu.VMEM((nz, both, units), bf16),
            pltpu.VMEM((nz, both, units), bf16),
            pltpu.VMEM((nz, both, units), bf16),
            pltpu.VMEM((2, nz, 2 * nz, 1, LANES), f32),
            pltpu.VMEM((2, 2 * both, units), f32),
            pltpu.VMEM((2, 2 * both, quarter), f32),
            pltpu.VMEM((nz, both, quarter), f32),
            pltpu.VMEM((nz, both, quarter), bf16),
            pltpu.VMEM((nz, both, quarter), bf16),
            pltpu.VMEM((nz - 1, both, quarter), bf16),
            pltpu.VMEM((nz, both, quarter), bf16),
            pltpu.VMEM((both, quarter), bf16),
            dma((sends,)),
            dma((11 + many,)),
            dma((2, 2, nz, pieces)),
            dma((2, nz)),
            dma((2,)),
            dma((nz,)),
            dma((nz, many)),
            dma((nz, many)),
            dma((3, many)),
        ],
        compiler_params=pltpu.CompilerParams(
            collective_id=0, has_side_effects=True, vmem_limit_bytes=48 * 1024 * 1024
        ),
    )(*(pltpu.with_memory_space_constraint(a, pltpu.HBM) for a in (tokens, gates.T, slots.T, plan, gate_proj, up_proj, down_proj)))


def body(tokens, gates, slots, plan, gate_proj, up_proj, down_proj):
    experts, attn = lax.axis_size("expert"), lax.axis_size("attn")
    tok, model = tokens.shape
    fits = (
        attn == 2 and experts % 2 == 0 and experts > 2
        and tok % ROWS == 0 and tok <= LANES
        and model % (4 * LANES) == 0 and gate_proj.shape[0] == 1
        and gate_proj.shape[2] % LANES == 0
    )
    chosen = fused_body if fits else dense_body
    return chosen(tokens, gates, slots, plan, gate_proj, up_proj, down_proj)


def solution(mesh):
    return jax.shard_map(
        body,
        mesh=mesh,
        in_specs=(
            P(("groups", "expert"), None),
            P(("groups", "expert"), None),
            P(("groups", "expert"), None),
            P("groups"),
            P("expert", None, "attn"),
            P("expert", None, "attn"),
            P("expert", None, "attn"),
        ),
        out_specs=P(("groups", "expert"), None),
        check_vma=False,
    )
```
